1024 devices in a mesh: seq: 32 (over z), tp: 8 (over y, core), dp: 4 (over x).
Axes of the slice: x: 4, y: 4, z: 32, core: 2. Of those that a mesh axis runs over, the one named last changes fastest.
Arguments:
- queries: bfloat16 [4, 4096, 8192], P('dp', 'seq', 'tp'), may hold values from -96 to 96
- images: bfloat16 [4, 32, 128, 8192], P('dp', 'seq', None, 'tp'), may hold values from -6 to 6
- kv_weight: bfloat16 [8192, 2048], P(None, 'tp'), may hold values from -0.0625 to 0.0625
- gate: float32 [1], replicated, may hold values from 0.3 to 1.5
- cotangent: bfloat16 [4, 4096, 8192], P('dp', 'seq', 'tp'), may hold values from -6 to 6
- span_first: int32 [4, 32], P('dp', 'seq'), may hold values from 0 to 30, as said below
- span_last: int32 [4, 32], P('dp', 'seq'), may hold values from 0 to 31, as said below
Outputs:
- attended: bfloat16 [4, 4096, 8192], P('dp', 'seq', 'tp')
- query_grad: bfloat16 [4, 4096, 8192], P('dp', 'seq', 'tp')
- weight_gradient: float32 [8192, 2048], P('seq', 'tp')
The draws below stay inside these ranges and needn't reach their ends.
Inputs may be any that keep to these rules, and one draw needn't show every extreme that they name: Text block b attends images span_first to span_last of its group, with b - 3 <= span_first <= span_last <= b; the last block of every group attends 4 images, and where 4 > 2 the block before it attends only its own image. `span_last`: see span_first.
All inputs are finite; a program needn't handle non-finite values.
Results may differ from the reference program's by a relative error of at most 0.03.
Values may be sent and summed in bfloat16 or wider, within the bound.
A program may use at most 32 MiB of HBM per device.

```python
import jax
import jax.numpy as jnp
from jax import lax

QUERY_HEADS = 64
VALUE_HEADS = 8
HEAD_SIZE = 128
STATE_WIDTH = 8192
TOKENS_PER_BLOCK = 128
IMAGE_PATCHES = 128
MOST_IMAGES = 4
GROUPS = 4
GROUP_IMAGES = 32
TEXT = 4096
KVW = 2048


def span_pair(key):
    key = jax.random.fold_in(key, 71)
    key_count, key_shift = jax.random.split(key)
    block_index = jnp.arange(GROUP_IMAGES, dtype=jnp.int32)[None, :]
    span_count = jax.random.randint(key_count, (GROUPS, GROUP_IMAGES), 1, MOST_IMAGES + 1)
    span_shift = jax.random.randint(key_shift, (GROUPS, GROUP_IMAGES), 0, MOST_IMAGES)
    span_end = jnp.maximum(block_index - span_shift, 0)
    lowest = jnp.maximum(block_index - MOST_IMAGES + 1, 0)
    span_start = jnp.maximum(span_end - span_count + 1, lowest)
    if MOST_IMAGES > 2:
        is_before = block_index == GROUP_IMAGES - 2
        span_start = jnp.where(is_before, GROUP_IMAGES - 2, span_start)
        span_end = jnp.where(is_before, GROUP_IMAGES - 2, span_end)
    is_final = block_index == GROUP_IMAGES - 1
    span_start = jnp.where(is_final, GROUP_IMAGES - MOST_IMAGES, span_start)
    span_end = jnp.where(is_final, GROUP_IMAGES - 1, span_end)
    return (span_start.astype(jnp.int32), span_end.astype(jnp.int32))


def draw_span_first(key, part):
    return span_pair(key)[0]


def draw_span_last(key, part):
    return span_pair(key)[1]


def draw_queries(key, part):
    values_raw = jnp.clip(jax.random.normal(key, (GROUPS, TEXT, QUERY_HEADS * HEAD_SIZE), jnp.float32), -6.0, 6.0)
    return values_raw.astype(jnp.bfloat16)


def level_of(stream_key, extent, cuts, smallest, largest):
    gain = 1.0
    for position, parts in cuts:
        steps = jax.random.uniform(jax.random.fold_in(jax.random.fold_in(stream_key, 6), position), (parts,), jnp.float32, smallest / len(cuts), largest / len(cuts))
        gain = gain * jnp.repeat(jnp.exp(steps), extent[position] // parts).reshape((-1,) + (1,) * (len(extent) - 1 - position))
    return gain


def bell_draw(stream_key, extent, deviation, reach, pieces=(), kind=jnp.bfloat16):
    values = deviation * jax.random.normal(stream_key, extent, jnp.float32)
    if pieces:
        values = values * level_of(stream_key, extent, pieces, -0.22, 0.18)
    return jnp.clip(values, -reach, reach).astype(kind)


def setup_inputs(seed: int = 0) -> dict:
    keys = jax.random.split(jax.random.key(seed), 8)
    return {
        "queries": draw_queries(jax.random.fold_in(keys[7], 71), 0),
        "images": bell_draw(keys[1], (GROUPS, GROUP_IMAGES, IMAGE_PATCHES, STATE_WIDTH), 1.0, 6.0, ((0, 4), (1, 32), (3, 8))),
        "kv_weight": bell_draw(keys[2], (STATE_WIDTH, KVW), STATE_WIDTH ** -0.5, 0.0625, ((1, 8),)),
        "gate": jnp.clip(jax.random.uniform(keys[3], (1,), jnp.float32, 0.3, 1.5), 0.3, 1.5),
        "cotangent": bell_draw(keys[4], (GROUPS, TEXT, QUERY_HEADS * HEAD_SIZE), 1.0, 6.0, ((0, 4), (1, 32), (2, 8))),
        "span_first": draw_span_first(jax.random.fold_in(keys[7], 71), 0),
        "span_last": draw_span_last(jax.random.fold_in(keys[7], 71), 0),
    }


def attend(query_rows, key_rows, value_rows, is_live, gate_tanh, cotangent_rows):
    hp = lax.Precision.HIGHEST
    scale = HEAD_SIZE ** -0.5
    query32 = query_rows.astype(jnp.float32)
    key32 = key_rows.astype(jnp.float32)
    value32 = value_rows.astype(jnp.float32)
    scores = jnp.einsum('tkgd,wpkd->kgtwp', query32, key32, precision=hp) * scale
    scores = jnp.where(is_live[None, None, None, :, None], scores, -jnp.inf)
    row_max = jnp.max(scores, axis=(3, 4), keepdims=True)
    exponent = jnp.exp(scores - row_max)
    attn_prob = exponent / jnp.sum(exponent, axis=(3, 4), keepdims=True)
    prob_low = attn_prob.astype(jnp.bfloat16)
    context = jnp.einsum('kgtwp,wpkd->tkgd', prob_low.astype(jnp.float32), value32, precision=hp)
    attended_rows = (gate_tanh * context).astype(jnp.bfloat16)
    d_context = (gate_tanh * cotangent_rows.astype(jnp.float32)).astype(jnp.bfloat16)
    d_context32 = d_context.astype(jnp.float32)
    row_delta = jnp.transpose(jnp.sum(d_context32 * context, axis=-1), (1, 2, 0))
    d_probs = jnp.einsum('tkgd,wpkd->kgtwp', d_context32, value32, precision=hp)
    d_scores = (attn_prob * (d_probs - row_delta[..., None, None]) * scale).astype(jnp.bfloat16)
    d_scores32 = d_scores.astype(jnp.float32)
    grad_query = jnp.einsum('kgtwp,wpkd->tkgd', d_scores32, key32, precision=hp).astype(jnp.bfloat16)
    grad_keys = jnp.einsum('kgtwp,tkgd->wpkd', d_scores32, query32, precision=hp)
    grad_values = jnp.einsum('kgtwp,tkgd->wpkd', prob_low.astype(jnp.float32), d_context32, precision=hp)
    return attended_rows, grad_query, grad_keys, grad_values


def image_summand(total, pair):
    image_rows, grad_rows = pair
    term = lax.dot_general(image_rows, grad_rows, (((0,), (0,)), ((), ())), preferred_element_type=jnp.float32)
    term = lax.optimization_barrier(term.astype(jnp.bfloat16))
    return total + term.astype(jnp.float32), None


def reference(queries, images, kv_weight, gate, cotangent, span_first, span_last):
    gate_tanh = jnp.tanh(gate[0])
    size_of_group = QUERY_HEADS // VALUE_HEADS
    attended_all = []
    query_all = []
    weight_gradient = jnp.zeros((STATE_WIDTH, 2 * VALUE_HEADS * HEAD_SIZE), jnp.float32)
    for index_of_group in range(GROUPS):
        flat_images = images[index_of_group].reshape(GROUP_IMAGES * IMAGE_PATCHES, STATE_WIDTH)
        key_value_pairs = jnp.dot(flat_images, kv_weight, preferred_element_type=jnp.float32).astype(jnp.bfloat16)
        key_value_pairs = key_value_pairs.reshape(GROUP_IMAGES, IMAGE_PATCHES, VALUE_HEADS, 2, HEAD_SIZE)
        padded_states = jnp.concatenate([jnp.zeros((MOST_IMAGES - 1, IMAGE_PATCHES, VALUE_HEADS, 2, HEAD_SIZE), jnp.bfloat16), key_value_pairs], 0)
        query_block_rows = queries[index_of_group].reshape(GROUP_IMAGES, TOKENS_PER_BLOCK, VALUE_HEADS, size_of_group, HEAD_SIZE)
        cotangent_block_rows = cotangent[index_of_group].reshape(GROUP_IMAGES, TOKENS_PER_BLOCK, VALUE_HEADS, size_of_group, HEAD_SIZE)

        def scan_step(running_total, scan_inputs):
            block_index, query_rows, cotangent_rows, span_start, span_end = scan_inputs
            window = lax.dynamic_slice_in_dim(padded_states, block_index, MOST_IMAGES, 0)
            image_index = block_index - MOST_IMAGES + 1 + jnp.arange(MOST_IMAGES, dtype=jnp.int32)
            is_live = (image_index >= span_start) & (image_index <= span_end)
            attended_rows, grad_query, grad_keys, grad_values = attend(
                query_rows, window[:, :, :, 0], window[:, :, :, 1], is_live, gate_tanh, cotangent_rows)
            grad_parts = jnp.stack([grad_keys, grad_values], 3)
            previous = lax.dynamic_slice_in_dim(running_total, block_index, MOST_IMAGES, 0)
            running_total = lax.dynamic_update_slice_in_dim(running_total, previous + grad_parts, block_index, 0)
            return running_total, (attended_rows, grad_query)

        zeroed_gradients = jnp.zeros((GROUP_IMAGES + MOST_IMAGES - 1, IMAGE_PATCHES, VALUE_HEADS, 2, HEAD_SIZE), jnp.float32)
        running_total, (attended_rows, grad_query) = lax.scan(
            scan_step, zeroed_gradients,
            (jnp.arange(GROUP_IMAGES, dtype=jnp.int32), query_block_rows, cotangent_block_rows, span_first[index_of_group], span_last[index_of_group]))
        key_value_gradient_bf = running_total[MOST_IMAGES - 1:].reshape(GROUP_IMAGES, IMAGE_PATCHES, 2 * VALUE_HEADS * HEAD_SIZE).astype(jnp.bfloat16)
        gradient_of_group, discarded_output = lax.scan(image_summand, jnp.zeros((STATE_WIDTH, 2 * VALUE_HEADS * HEAD_SIZE), jnp.float32),
                                      (images[index_of_group], key_value_gradient_bf))
        weight_gradient = weight_gradient + gradient_of_group
        attended_all.append(attended_rows.reshape(TEXT, QUERY_HEADS * HEAD_SIZE))
        query_all.append(grad_query.reshape(TEXT, QUERY_HEADS * HEAD_SIZE))
    return jnp.stack(attended_all), jnp.stack(query_all), weight_gradient
```

```python
import functools

import jax
import jax.numpy as jnp
from jax import lax
from jax.experimental import pallas as pl
from jax.experimental.pallas import tpu as pltpu
from jax.sharding import PartitionSpec as P

HEADS = 8
HEAD_SIZE = 128
TOKENS = 128
PATCHES = 128
REACH = 4
TP = 8
DP = 4
SHARD = 1024
HALF = SHARD // 2
KVC = 2 * HEAD_SIZE
SCALE = HEAD_SIZE ** (-0.5)
GATHER_COPIES = 14
PARTS = 2

BF16 = jnp.bfloat16
F32 = jnp.float32


def remote(src, dst, send_sem, recv_sem, **where):
    return pltpu.make_async_remote_copy(
        src_ref=src,
        dst_ref=dst,
        send_sem=send_sem,
        recv_sem=recv_sem,
        device_id=where,
        device_id_type=pl.DeviceIdType.MESH,
    )


class RowGather:
    def __init__(self, own, slot, send_sems, recv_sems):
        tp = lax.axis_index("tp")
        self.tp = tp
        self.right, self.left = lax.rem(tp + 2, TP), lax.rem(tp + TP - 2, TP)
        self.opposite = lax.rem(tp + 4, TP)
        self.sibling = tp + 1 - 2 * lax.rem(tp, 2)
        self.own, self.slot = own, slot
        self.send_sems, self.recv_sems = send_sems, recv_sems
        self.started = []

    def _copy(self, index, src, dst, target):
        return remote(src, dst, self.send_sems.at[index], self.recv_sems.at[index], tp=target)

    def _start(self, index, src, owner, half, target):
        copy = self._copy(index, src, self.slot(owner, half), target)
        copy.start()
        self.started.append(copy)

    def _arrived(self, index, owner, half):
        ref = self.slot(owner, half)
        self._copy(index, ref, ref, self.right).wait_recv()

    def send_own(self):
        for half in (0, 1):
            self._start(half, self.own(half), self.tp, half, self.right)
            self._start(3 - half, self.own(1 - half), self.tp, 1 - half, self.left)
        for half in (0, 1):
            self._start(6 + half, self.own(half), self.tp, half, self.sibling)

    def sibling_own(self, half):
        self._arrived(6 + half, self.sibling, half)
        return self.sibling, half

    def from_left(self, half):
        self._arrived(half, self.left, half)
        ref = self.slot(self.left, half)
        if half == 0:
            self._start(4, ref, self.left, half, self.right)
        self._start(8 + half, ref, self.left, half, self.sibling)
        return self.left, half

    def from_right(self, half):
        self._arrived(2 + half, self.right, half)
        ref = self.slot(self.right, half)
        if half == 1:
            self._start(5, ref, self.right, half, self.left)
        self._start(10 + half, ref, self.right, half, self.sibling)
        return self.right, half

    def from_opposite(self, half):
        self._arrived(4 + half, self.opposite, half)
        self._start(12 + half, self.slot(self.opposite, half), self.opposite, half, self.sibling)
        return self.opposite, half

    def sibling_other(self, which, half):
        owner = lax.rem(self.sibling + (TP - 2, 2, 4)[which], TP)
        self._arrived(8 + 2 * which + half, owner, half)
        return owner, half

    def finish(self):
        for copy in self.started:
            copy.wait_send()


def kernel(
    nz,
    queries,
    features,
    kv_weight,
    gate,
    cotangent,
    span_first,
    span_last,
    attended_out,
    query_grad_out,
    weight_out,
    q_buf,
    cot_buf,
    w_buf,
    gathered,
    proj,
    transposed,
    columns,
    q_t,
    dc_buf,
    dc_t,
    keys,
    values,
    scores,
    d_probs,
    p_buf,
    ds_buf,
    att_buf,
    dq_buf,
    part,
    chain_out,
    chain_in,
    dkv,
    term,
    ring_out,
    ring_in,
    quarter,
    local_sems,
    feat_send,
    feat_recv,
    col_send,
    col_recv,
    cross_send,
    cross_recv,
    kv_send,
    kv_recv,
    chain_send,
    chain_recv,
    dkv_send,
    dkv_recv,
    ring_send,
    ring_recv,
    last_send,
    last_recv,
):
    z, tp, dp = lax.axis_index("seq"), lax.axis_index("tp"), lax.axis_index("dp")
    z_next, z_prev = lax.rem(z + 1, nz), lax.rem(z + nz - 1, nz)

    w_copies = []
    in_q = pltpu.make_async_copy(queries.at[0], q_buf, local_sems.at[0])
    in_cot = pltpu.make_async_copy(cotangent.at[0], cot_buf, local_sems.at[1])
    in_w = pltpu.make_async_copy(kv_weight, w_buf, local_sems.at[2])
    in_q.start()
    in_cot.start()
    in_w.start()

    gather = RowGather(
        lambda half: features.at[0, 0, :, pl.ds(half * HALF, HALF)],
        lambda owner, half: gathered.at[owner, :, pl.ds(half * HALF, HALF)],
        feat_send,
        feat_recv,
    )
    barrier = pltpu.get_barrier_semaphore()
    mesh_id = pl.DeviceIdType.MESH
    for other in (gather.right, gather.left, gather.sibling):
        pl.semaphore_signal(barrier, inc=1, device_id={"tp": other}, device_id_type=mesh_id)
    for steps in range(1, DP):
        other = lax.rem(dp + steps, DP)
        pl.semaphore_signal(barrier, inc=1, device_id={"dp": other}, device_id_type=mesh_id)
    for other in (z_next, z_prev):
        pl.semaphore_signal(barrier, inc=1, device_id={"seq": other}, device_id_type=mesh_id)
    pl.semaphore_wait(barrier, 8)

    gather.send_own()

    for block in range(SHARD // 128):
        tile = features[0, 0, :, block * 128 : (block + 1) * 128].astype(F32)
        flipped = jnp.transpose(tile).astype(BF16)
        for piece in range(2):
            place = block * 2 + piece
            transposed[place // 4, place % 4] = flipped[piece * 64 : (piece + 1) * 64]
    own_quarter = pltpu.make_async_copy(
        transposed.at[:, dp], columns.at[tp, :, :, pl.ds(0, 128)], local_sems.at[3]
    )
    own_quarter.start()
    cross = []
    for steps in range(1, DP):
        to = lax.rem(dp + steps, DP)
        copy = remote(
            transposed.at[:, to],
            columns.at[tp, :, :, pl.ds(steps * 128, 128)],
            cross_send.at[steps - 1],
            cross_recv.at[steps - 1],
            dp=to,
        )
        copy.start()
        cross.append(copy)

    in_w.wait()

    def project(owner, half, block=None):
        rows = pl.ds(pl.multiple_of(owner * SHARD + half * HALF, HALF), HALF)
        block = gathered[owner, :, half * HALF : (half + 1) * HALF] if block is None else block
        return jnp.dot(block, w_buf[rows, :], preferred_element_type=F32)

    proj[...] = project(tp, 0, features[0, 0, :, :HALF]) + project(tp, 1, features[0, 0, :, HALF:])
    for half in (0, 1):
        proj[...] += project(*gather.sibling_own(half))

    in_q.wait()
    in_cot.wait()
    gate_tanh = jnp.tanh(jnp.full((8, 128), gate[0], F32))[:1]

    def prepare(head, _):
        lanes = pl.ds(pl.multiple_of(head * HEAD_SIZE, HEAD_SIZE), HEAD_SIZE)
        low = (gate_tanh * cot_buf[:, lanes].astype(F32)).astype(BF16)
        dc_buf[:, lanes] = low
        dc_t[:, lanes] = jnp.transpose(low.astype(F32)).astype(BF16)
        q_t[:, lanes] = jnp.transpose(q_buf[:, lanes].astype(F32)).astype(BF16)
        return 0

    lax.fori_loop(0, HEADS, prepare, 0)

    arrived = [gather.from_left(0), gather.from_right(1)]
    for owner, half in arrived:
        proj[...] += project(owner, half)
    arrived = [gather.from_left(1), gather.from_right(0)]
    for owner, half in arrived:
        proj[...] += project(owner, half)
    for which, half in ((0, 0), (1, 1), (0, 1), (1, 0)):
        proj[...] += project(*gather.sibling_other(which, half))
    arrived = [gather.from_opposite(0), gather.from_opposite(1)]
    for owner, half in arrived:
        proj[...] += project(owner, half)
    for half in (0, 1):
        proj[...] += project(*gather.sibling_other(2, half))

    keys[pl.ds(0, PATCHES), :] = proj[:, :HEAD_SIZE].astype(BF16)
    values[pl.ds(0, PATCHES), :] = proj[:, HEAD_SIZE:].astype(BF16)

    halo = []

    def pass_on(offset):
        for side, rows in enumerate((keys, values)):
            copy = remote(
                rows.at[pl.ds(offset * PATCHES, PATCHES), :],
                rows.at[pl.ds((offset + 1) * PATCHES, PATCHES), :],
                kv_send.at[offset * 2 + side],
                kv_recv.at[offset * 2 + side],
                seq=z_next,
            )
            copy.start()
            halo.append(copy)

    pass_on(0)

    own_quarter.wait()
    for copy in cross:
        copy.wait_recv()
    second = RowGather(
        lambda half: columns.at[tp, pl.ds(half * 2, 2)],
        lambda owner, half: columns.at[owner, pl.ds(half * 2, 2)],
        col_send,
        col_recv,
    )
    second.send_own()

    def score(offset):
        rows = pl.ds(offset * PATCHES, PATCHES)
        nt = (((1,), (1,)), ((), ()))

        def one(head, _):
            lanes = pl.ds(pl.multiple_of(head * HEAD_SIZE, HEAD_SIZE), HEAD_SIZE)
            scores[head, :, rows] = lax.dot_general(
                q_buf[:, lanes], keys[rows, :], nt, preferred_element_type=F32
            )
            d_probs[head, :, rows] = lax.dot_general(
                dc_buf[:, lanes], values[rows, :], nt, preferred_element_type=F32
            )
            return 0

        lax.fori_loop(0, HEADS, one, 0)

    score(0)
    for offset in range(1, REACH):
        for copy in halo[2 * offset - 2 : 2 * offset]:
            copy.wait_recv()
        if offset < REACH - 1:
            pass_on(offset)
        score(offset)

    second.from_left(0)
    second.from_right(1)
    second.from_left(1)
    second.from_right(0)

    lane = lax.broadcasted_iota(jnp.int32, (1, REACH * PATCHES), 1)
    image = z - lax.div(lane, PATCHES)
    is_live = (image >= span_first[0, 0]) & (image <= span_last[0, 0])
    bias = jnp.where(is_live, 0.0, -jnp.inf).astype(F32)

    def attend(head, _):
        lanes = pl.ds(pl.multiple_of(head * HEAD_SIZE, HEAD_SIZE), HEAD_SIZE)
        rows = pl.ds(pl.multiple_of(head * TOKENS, TOKENS), TOKENS)
        logits = scores[head] * SCALE + bias
        exponent = jnp.exp(logits - jnp.max(logits, axis=1, keepdims=True))
        prob = exponent / jnp.sum(exponent, axis=1, keepdims=True)
        prob_low = prob.astype(BF16)
        context = jnp.dot(prob_low, values[...], preferred_element_type=F32)
        att_buf[:, lanes] = (gate_tanh * context).astype(BF16)
        delta = jnp.sum(dc_buf[:, lanes].astype(F32) * context, axis=1, keepdims=True)
        d_score = (prob * (d_probs[head] - delta) * SCALE).astype(BF16)
        dq_buf[:, lanes] = jnp.dot(d_score, keys[...], preferred_element_type=F32).astype(BF16)
        p_buf[rows, :] = prob_low
        ds_buf[rows, :] = d_score
        return 0

    lax.fori_loop(0, HEADS, attend, 0)
    out_att = pltpu.make_async_copy(att_buf, attended_out.at[0], local_sems.at[4])
    out_dq = pltpu.make_async_copy(dq_buf, query_grad_out.at[0], local_sems.at[5])
    out_att.start()
    out_dq.start()

    def partial_gradients(pair):
        window = pl.ds(pair * 2 * PATCHES, 2 * PATCHES)
        for side, (left_ref, right_ref) in enumerate(((q_t, ds_buf), (dc_t, p_buf))):
            both = jnp.dot(left_ref[...], right_ref[:, window], preferred_element_type=F32)
            for index in range(2):
                tile = both[:, index * PATCHES : (index + 1) * PATCHES]
                part[pair * 2 + index, side] = jnp.transpose(tile)

    chain = []

    def hand_back(step):
        for side in range(2):
            copy = remote(
                chain_out.at[step, side],
                chain_in.at[step, side],
                chain_send.at[step * 2 + side],
                chain_recv.at[step * 2 + side],
                seq=z_prev,
            )
            copy.start()
            chain.append(copy)

    partial_gradients(1)
    chain_out[0] = part[REACH - 1].astype(BF16)
    hand_back(0)
    partial_gradients(0)
    second.from_opposite(0)
    second.from_opposite(1)
    for step in range(1, REACH):
        for side in range(2):
            chain[2 * step - 2 + side].wait_recv()
        total = part[REACH - 1 - step] + chain_in[step - 1].astype(F32)
        if step < REACH - 1:
            chain_out[step] = total.astype(BF16)
            hand_back(step)
        else:
            dkv[pl.ds(0, PATCHES), pl.ds(0, HEAD_SIZE)] = total[0].astype(BF16)
            dkv[pl.ds(0, PATCHES), pl.ds(HEAD_SIZE, HEAD_SIZE)] = total[1].astype(BF16)

    shared = []
    for steps in range(1, DP):
        copy = remote(
            dkv.at[pl.ds(0, PATCHES), :],
            dkv.at[pl.ds(steps * PATCHES, PATCHES), :],
            dkv_send.at[steps - 1],
            dkv_recv.at[steps - 1],
            dp=lax.rem(dp + steps, DP),
        )
        copy.start()
        shared.append(copy)
    for half in (0, 1):
        second.sibling_own(half)
        for which in range(3):
            second.sibling_other(which, half)
    for copy in shared:
        copy.wait_recv()

    zs = nz // TP

    def make_term(turn):
        owner = lax.rem(lax.div(z, zs) + turn, TP)
        rows = columns[owner].reshape(zs * 64, DP * PATCHES)
        result = jnp.dot(rows, dkv[...], preferred_element_type=F32)
        term[pl.ds(owner * zs, zs)] = result.reshape(zs, 64, KVC)

    far = nz // 2
    height = 64 // PARTS

    def ring_copy(way, step, piece):
        index = (way * far + step) * PARTS + piece
        rows = pl.ds(piece * height, height)
        return remote(
            ring_out.at[way, step, rows, :],
            ring_in.at[way, step, rows, :],
            ring_send.at[index],
            ring_recv.at[index],
            seq=(z_next, z_prev)[way],
        )

    def target(way, step):
        return lax.rem((z + far - step, z + far + 1 + step)[way], nz)

    make_term(4)
    make_term(5)
    for way in range(2):
        ring_out[way, 0] = term[target(way, 0)].astype(BF16)
        for piece in range(PARTS):
            ring_copy(way, 0, piece).start()
    for turn in (3, 6, 2, 7, 1, 0):
        make_term(turn)

    def ring_step(step, ways):
        for piece in range(PARTS):
            rows = pl.ds(piece * height, height)
            for way in ways:
                ring_copy(way, step - 1, piece).wait_recv()
                total = ring_in[way, step - 1, rows, :].astype(F32) + term[target(way, step), rows, :]
                ring_out[way, step, rows, :] = total.astype(BF16)
                ring_copy(way, step, piece).start()

    def both_ways(step, _):
        ring_step(step, (0, 1))
        return 0

    lax.fori_loop(1, far - 1, both_ways, 0)
    ring_step(far - 1, (0,))

    for piece in range(PARTS):
        ring_copy(0, far - 1, piece).wait_recv()
        ring_copy(1, far - 2, piece).wait_recv()
    total = ring_in[0, far - 1].astype(F32) + ring_in[1, far - 2].astype(F32) + term[z]
    quarter[dp] = total
    last = []
    for steps in range(1, DP):
        copy = remote(
            quarter.at[dp],
            quarter.at[dp],
            last_send.at[steps - 1],
            last_recv.at[steps - 1],
            dp=lax.rem(dp + steps, DP),
        )
        copy.start()
        last.append(copy)

    gather.finish()
    second.finish()
    for copy in cross + halo + chain + shared:
        copy.wait_send()

    def ring_sent(step, _):
        for way in range(2):
            for piece in range(PARTS):
                ring_copy(way, step, piece).wait_send()
        return 0

    lax.fori_loop(0, far - 1, ring_sent, 0)
    for piece in range(PARTS):
        ring_copy(0, far - 1, piece).wait_send()
    out_att.wait()
    out_dq.wait()
    for steps in range(1, DP):
        source = lax.rem(dp + DP - steps, DP)
        remote(
            quarter.at[source],
            quarter.at[source],
            last_send.at[steps - 1],
            last_recv.at[steps - 1],
            dp=source,
        ).wait_recv()
    for copy in last:
        copy.wait_send()
    weight_out[...] = quarter[...].reshape(DP * 64, KVC)


def local(nz, queries, images, kv_weight, gate, cotangent, span_first, span_last):
    far = nz // 2
    zs = nz // TP
    any_space = pl.BlockSpec(memory_space=pl.ANY)
    vmem = pl.BlockSpec(memory_space=pltpu.VMEM)
    smem = pl.BlockSpec(memory_space=pltpu.SMEM)
    dma = pltpu.SemaphoreType.DMA
    rows = REACH * PATCHES
    low = lambda *shape: pltpu.VMEM(shape, BF16)
    wide = lambda *shape: pltpu.VMEM(shape, F32)
    return pl.pallas_call(
        functools.partial(kernel, nz),
        out_shape=(
            jax.ShapeDtypeStruct(queries.shape, BF16),
            jax.ShapeDtypeStruct(queries.shape, BF16),
            jax.ShapeDtypeStruct((DP * 64, KVC), F32),
        ),
        in_specs=[any_space, vmem, any_space, smem, any_space, smem, smem],
        out_specs=(any_space, any_space, vmem),
        scratch_shapes=[
            low(TOKENS, SHARD),
            low(TOKENS, SHARD),
            low(TP * SHARD, KVC),
            low(TP, PATCHES, SHARD),
            wide(PATCHES, KVC),
            low(zs, DP, 64, PATCHES),
            low(TP, zs, 64, DP * PATCHES),
            low(HEAD_SIZE, SHARD),
            low(TOKENS, SHARD),
            low(HEAD_SIZE, SHARD),
            low(rows, HEAD_SIZE),
            low(rows, HEAD_SIZE),
            wide(HEADS, TOKENS, rows),
            wide(HEADS, TOKENS, rows),
            low(HEADS * TOKENS, rows),
            low(HEADS * TOKENS, rows),
            low(TOKENS, SHARD),
            low(TOKENS, SHARD),
            wide(REACH, 2, PATCHES, HEAD_SIZE),
            low(REACH - 1, 2, PATCHES, HEAD_SIZE),
            low(REACH - 1, 2, PATCHES, HEAD_SIZE),
            low(DP * PATCHES, KVC),
            wide(nz, 64, KVC),
            low(2, far, 64, KVC),
            low(2, far, 64, KVC),
            wide(DP, 64, KVC),
            dma((6,)),
            dma((GATHER_COPIES,)),
            dma((GATHER_COPIES,)),
            dma((GATHER_COPIES,)),
            dma((GATHER_COPIES,)),
            dma((DP - 1,)),
            dma((DP - 1,)),
            dma((2 * (REACH - 1),)),
            dma((2 * (REACH - 1),)),
            dma((2 * (REACH - 1),)),
            dma((2 * (REACH - 1),)),
            dma((DP - 1,)),
            dma((DP - 1,)),
            dma((2 * far * PARTS,)),
            dma((2 * far * PARTS,)),
            dma((DP - 1,)),
            dma((DP - 1,)),
        ],
        compiler_params=pltpu.CompilerParams(
            collective_id=0, has_side_effects=True, vmem_limit_bytes=48 * 1024 * 1024
        ),
        name="cross_attention",
    )(queries, images, kv_weight, gate, cotangent, span_first, span_last)


def solution(mesh):
    return jax.shard_map(
        functools.partial(local, mesh.shape["seq"]),
        mesh=mesh,
        in_specs=(
            P("dp", "seq", "tp"),
            P("dp", "seq", None, "tp"),
            P(None, "tp"),
            P(),
            P("dp", "seq", "tp"),
            P("dp", "seq"),
            P("dp", "seq"),
        ),
        out_specs=(P("dp", "seq", "tp"), P("dp", "seq", "tp"), P("seq", "tp")),
        check_vma=False,
    )
```

```python
import functools

import jax
import jax.numpy as jnp
from jax import lax
from jax.experimental import pallas as pl
from jax.experimental.pallas import tpu as pltpu
from jax.sharding import PartitionSpec as P

HEADS = 8
HEAD_SIZE = 128
TOKENS = 128
PATCHES = 128
REACH = 4
TP = 8
DP = 4
SHARD = 1024
HALF = SHARD // 2
KVC = 2 * HEAD_SIZE
SCALE = HEAD_SIZE ** (-0.5)
GATHER_COPIES = 14
GREETINGS = (1, 2, 4, 4)
STRETCHES = ((9, 7), (8, 7))
PARTS = 2

BF16 = jnp.bfloat16
F32 = jnp.float32


def remote(src, dst, send_sem, recv_sem, **where):
    return pltpu.make_async_remote_copy(
        src_ref=src,
        dst_ref=dst,
        send_sem=send_sem,
        recv_sem=recv_sem,
        device_id=where,
        device_id_type=pl.DeviceIdType.MESH,
    )


def ring_lanes(nz):
    lanes, slot = [], 0
    for way in range(2):
        base = 0
        for size in STRETCHES[way]:
            lanes.append((way, base, size, slot))
            base, slot = base + size, slot + size
        assert base == nz // 2 - way
    return sorted(lanes, key=lambda lane: -lane[1] - lane[2])


class RowGather:
    def __init__(self, own, slot, send_sems, recv_sems):
        tp = lax.axis_index("tp")
        self.tp = tp
        self.right, self.left = lax.rem(tp + 2, TP), lax.rem(tp + TP - 2, TP)
        self.opposite = lax.rem(tp + 4, TP)
        self.sibling = tp + 1 - 2 * lax.rem(tp, 2)
        self.own, self.slot = own, slot
        self.send_sems, self.recv_sems = send_sems, recv_sems
        self.started = []

    def _copy(self, index, src, dst, target):
        return remote(src, dst, self.send_sems.at[index], self.recv_sems.at[index], tp=target)

    def _start(self, index, src, owner, half, target):
        copy = self._copy(index, src, self.slot(owner, half), target)
        copy.start()
        self.started.append(copy)

    def _arrived(self, index, owner, half):
        ref = self.slot(owner, half)
        self._copy(index, ref, ref, self.right).wait_recv()

    def send_own(self):
        for half in (0, 1):
            self._start(half, self.own(half), self.tp, half, self.right)
            self._start(3 - half, self.own(1 - half), self.tp, 1 - half, self.left)
        for half in (0, 1):
            self._start(6 + half, self.own(half), self.tp, half, self.sibling)

    def sibling_own(self, half):
        self._arrived(6 + half, self.sibling, half)
        return self.sibling, half

    def from_left(self, half):
        self._arrived(half, self.left, half)
        ref = self.slot(self.left, half)
        if half == 0:
            self._start(4, ref, self.left, half, self.right)
        self._start(8 + half, ref, self.left, half, self.sibling)
        return self.left, half

    def from_right(self, half):
        self._arrived(2 + half, self.right, half)
        ref = self.slot(self.right, half)
        if half == 1:
            self._start(5, ref, self.right, half, self.left)
        self._start(10 + half, ref, self.right, half, self.sibling)
        return self.right, half

    def from_opposite(self, half):
        self._arrived(4 + half, self.opposite, half)
        self._start(12 + half, self.slot(self.opposite, half), self.opposite, half, self.sibling)
        return self.opposite, half

    def sibling_other(self, which, half):
        owner = lax.rem(self.sibling + (TP - 2, 2, 4)[which], TP)
        self._arrived(8 + 2 * which + half, owner, half)
        return owner, half

    def finish(self):
        for copy in self.started:
            copy.wait_send()


def kernel(
    nz,
    queries,
    features,
    kv_weight,
    gate,
    cotangent,
    span_first,
    span_last,
    attended_out,
    query_grad_out,
    weight_out,
    q_buf,
    cot_buf,
    w_buf,
    gathered,
    proj,
    transposed,
    columns,
    q_t,
    dc_buf,
    dc_t,
    keys,
    values,
    scores,
    d_probs,
    p_buf,
    ds_buf,
    att_buf,
    dq_buf,
    part,
    chain_out,
    chain_in,
    dkv,
    term,
    ring_out,
    ring_in,
    quarter,
    local_sems,
    feat_send,
    feat_recv,
    col_send,
    col_recv,
    cross_send,
    cross_recv,
    kv_send,
    kv_recv,
    chain_send,
    chain_recv,
    dkv_send,
    dkv_recv,
    ring_send,
    ring_recv,
    last_send,
    last_recv,
    greeted,
):
    z, tp, dp = lax.axis_index("seq"), lax.axis_index("tp"), lax.axis_index("dp")
    z_next, z_prev = lax.rem(z + 1, nz), lax.rem(z + nz - 1, nz)

    in_q = pltpu.make_async_copy(queries.at[0], q_buf, local_sems.at[0])
    in_cot = pltpu.make_async_copy(cotangent.at[0], cot_buf, local_sems.at[1])
    in_w = pltpu.make_async_copy(kv_weight, w_buf, local_sems.at[2])
    in_f = pltpu.make_async_copy(features.at[0, 0], gathered.at[lax.axis_index('tp')], local_sems.at[6])
    in_f.start()
    in_q.start()
    in_cot.start()
    in_w.start()

    gather = RowGather(
        lambda half: features.at[0, 0, :, pl.ds(half * HALF, HALF)],
        lambda owner, half: gathered.at[owner, :, pl.ds(half * HALF, HALF)],
        feat_send,
        feat_recv,
    )
    barrier = pltpu.get_barrier_semaphore()
    mesh_id = pl.DeviceIdType.MESH
    for other in (gather.right, gather.left, gather.sibling):
        pl.semaphore_signal(barrier, inc=1, device_id={"tp": other}, device_id_type=mesh_id)
    for steps in range(1, DP):
        other = lax.rem(dp + steps, DP)
        pl.semaphore_signal(barrier, inc=1, device_id={"dp": other}, device_id_type=mesh_id)
    for other in (z_next, z_prev):
        pl.semaphore_signal(barrier, inc=1, device_id={"seq": other}, device_id_type=mesh_id)
    pl.semaphore_wait(barrier, 8)

    def greet(turn):
        for way in range(2):
            step = GREETINGS[turn]
            other = lax.rem((z + step, z + nz - step)[way], nz)
            pl.semaphore_signal(greeted.at[turn * 2 + way], inc=1, device_id={"seq": other}, device_id_type=mesh_id)

    def heard(turn):
        for way in range(2):
            pl.semaphore_wait(greeted.at[turn * 2 + way], 1)

    gather.send_own()
    greet(0)
    in_f.wait()

    for block in range(SHARD // 128):
        tile = gathered[tp, :, block * 128 : (block + 1) * 128].astype(F32)
        flipped = jnp.transpose(tile).astype(BF16)
        for piece in range(2):
            place = block * 2 + piece
            transposed[place // 4, place % 4] = flipped[piece * 64 : (piece + 1) * 64]
    own_quarter = pltpu.make_async_copy(
        transposed.at[:, dp], columns.at[tp, :, :, pl.ds(0, 128)], local_sems.at[3]
    )
    own_quarter.start()
    cross = []
    for steps in range(1, DP):
        to = lax.rem(dp + steps, DP)
        copy = remote(
            transposed.at[:, to],
            columns.at[tp, :, :, pl.ds(steps * 128, 128)],
            cross_send.at[steps - 1],
            cross_recv.at[steps - 1],
            dp=to,
        )
        copy.start()
        cross.append(copy)

    in_w.wait()

    def project(owner, half):
        rows = pl.ds(pl.multiple_of(owner * SHARD + half * HALF, HALF), HALF)
        block = gathered[owner, :, half * HALF : (half + 1) * HALF]
        return jnp.dot(block, w_buf[rows, :], preferred_element_type=F32)

    proj[...] = project(tp, 0) + project(tp, 1)
    for half in (0, 1):
        proj[...] += project(*gather.sibling_own(half))

    in_q.wait()
    in_cot.wait()
    gate_tanh = jnp.tanh(jnp.full((8, 128), gate[0], F32))[:1]

    def prepare(head, _):
        lanes = pl.ds(pl.multiple_of(head * HEAD_SIZE, HEAD_SIZE), HEAD_SIZE)
        low = (gate_tanh * cot_buf[:, lanes].astype(F32)).astype(BF16)
        dc_buf[:, lanes] = low
        dc_t[:, lanes] = jnp.transpose(low.astype(F32)).astype(BF16)
        q_t[:, lanes] = jnp.transpose(q_buf[:, lanes].astype(F32)).astype(BF16)
        return 0

    lax.fori_loop(0, HEADS, prepare, 0)
    heard(0)
    greet(1)

    arrived = [gather.from_left(0), gather.from_right(1)]
    for owner, half in arrived:
        proj[...] += project(owner, half)
    arrived = [gather.from_left(1), gather.from_right(0)]
    for owner, half in arrived:
        proj[...] += project(owner, half)
    for which, half in ((0, 0), (1, 1), (0, 1), (1, 0)):
        proj[...] += project(*gather.sibling_other(which, half))
    arrived = [gather.from_opposite(0), gather.from_opposite(1)]
    for owner, half in arrived:
        proj[...] += project(owner, half)
    for half in (0, 1):
        proj[...] += project(*gather.sibling_other(2, half))

    keys[pl.ds(0, PATCHES), :] = proj[:, :HEAD_SIZE].astype(BF16)
    values[pl.ds(0, PATCHES), :] = proj[:, HEAD_SIZE:].astype(BF16)

    z_after, z_before = lax.rem(z + 2, nz), lax.rem(z + nz - 2, nz)
    halo = []

    def pass_on(source, offset, to):
        for side, rows in enumerate((keys, values)):
            copy = remote(
                rows.at[pl.ds(source * PATCHES, PATCHES), :],
                rows.at[pl.ds(offset * PATCHES, PATCHES), :],
                kv_send.at[offset * 2 - 2 + side],
                kv_recv.at[offset * 2 - 2 + side],
                seq=to,
            )
            copy.start()
            halo.append(copy)

    pass_on(0, 2, z_after)
    pass_on(0, 1, z_next)

    own_quarter.wait()
    for copy in cross:
        copy.wait_recv()
    second = RowGather(
        lambda half: columns.at[tp, pl.ds(half * 2, 2)],
        lambda owner, half: columns.at[owner, pl.ds(half * 2, 2)],
        col_send,
        col_recv,
    )
    second.send_own()

    def score(offset):
        rows = pl.ds(offset * PATCHES, PATCHES)
        nt = (((1,), (1,)), ((), ()))

        def one(head, _):
            lanes = pl.ds(pl.multiple_of(head * HEAD_SIZE, HEAD_SIZE), HEAD_SIZE)
            scores[head, :, rows] = lax.dot_general(
                q_buf[:, lanes], keys[rows, :], nt, preferred_element_type=F32
            )
            d_probs[head, :, rows] = lax.dot_general(
                dc_buf[:, lanes], values[rows, :], nt, preferred_element_type=F32
            )
            return 0

        lax.fori_loop(0, HEADS, one, 0)

    heard(1)
    greet(2)
    score(0)
    for copy in halo[:2]:
        copy.wait_recv()
    pass_on(2, 3, z_next)
    score(2)
    for copy in halo[2:4]:
        copy.wait_recv()
    score(1)
    for copy in halo[4:]:
        copy.wait_recv()
    score(3)

    second.from_left(0)
    second.from_right(1)
    second.from_left(1)
    second.from_right(0)

    lane = lax.broadcasted_iota(jnp.int32, (1, REACH * PATCHES), 1)
    image = z - lax.div(lane, PATCHES)
    is_live = (image >= span_first[0, 0]) & (image <= span_last[0, 0])
    bias = jnp.where(is_live, 0.0, -jnp.inf).astype(F32)

    def attend(head, _):
        lanes = pl.ds(pl.multiple_of(head * HEAD_SIZE, HEAD_SIZE), HEAD_SIZE)
        rows = pl.ds(pl.multiple_of(head * TOKENS, TOKENS), TOKENS)
        logits = scores[head] * SCALE + bias
        exponent = jnp.exp(logits - jnp.max(logits, axis=1, keepdims=True))
        prob = exponent * (1.0 / jnp.sum(exponent, axis=1, keepdims=True))
        prob_low = prob.astype(BF16)
        context = jnp.dot(prob_low, values[...], preferred_element_type=F32)
        att_buf[:, lanes] = (gate_tanh * context).astype(BF16)
        delta = jnp.sum(dc_buf[:, lanes].astype(F32) * context, axis=1, keepdims=True)
        d_score = (prob * (d_probs[head] - delta) * SCALE).astype(BF16)
        dq_buf[:, lanes] = jnp.dot(d_score, keys[...], preferred_element_type=F32).astype(BF16)
        p_buf[rows, :] = prob_low
        ds_buf[rows, :] = d_score
        return 0

    heard(2)
    greet(3)
    lax.fori_loop(0, HEADS, attend, 0)
    out_att = pltpu.make_async_copy(att_buf, attended_out.at[0], local_sems.at[4])
    out_dq = pltpu.make_async_copy(dq_buf, query_grad_out.at[0], local_sems.at[5])
    out_att.start()
    out_dq.start()

    def partial_gradients(pair):
        window = pl.ds(pair * 2 * PATCHES, 2 * PATCHES)
        for side, (left_ref, right_ref) in enumerate(((q_t, ds_buf), (dc_t, p_buf))):
            both = jnp.dot(left_ref[...], right_ref[:, window], preferred_element_type=F32)
            for index in range(2):
                tile = both[:, index * PATCHES : (index + 1) * PATCHES]
                part[pair * 2 + index, side] = jnp.transpose(tile)

    chain = []

    def hand_back(step, to):
        for side in range(2):
            copy = remote(
                chain_out.at[step, side],
                chain_in.at[step, side],
                chain_send.at[step * 2 + side],
                chain_recv.at[step * 2 + side],
                seq=to,
            )
            copy.start()
            chain.append(copy)

    partial_gradients(1)
    chain_out[0] = part[3].astype(BF16)
    hand_back(0, z_prev)
    partial_gradients(0)
    chain_out[2] = part[1].astype(BF16)
    hand_back(2, z_prev)
    second.from_opposite(0)
    second.from_opposite(1)
    for copy in chain[:2]:
        copy.wait_recv()
    chain_out[1] = (part[2] + chain_in[0].astype(F32)).astype(BF16)
    hand_back(1, z_before)
    for copy in chain[2:]:
        copy.wait_recv()
    total = part[0] + chain_in[2].astype(F32) + chain_in[1].astype(F32)
    dkv[pl.ds(0, PATCHES), pl.ds(0, HEAD_SIZE)] = total[0].astype(BF16)
    dkv[pl.ds(0, PATCHES), pl.ds(HEAD_SIZE, HEAD_SIZE)] = total[1].astype(BF16)

    shared = []
    for steps in range(1, DP):
        copy = remote(
            dkv.at[pl.ds(0, PATCHES), :],
            dkv.at[pl.ds(steps * PATCHES, PATCHES), :],
            dkv_send.at[steps - 1],
            dkv_recv.at[steps - 1],
            dp=lax.rem(dp + steps, DP),
        )
        copy.start()
        shared.append(copy)
    for half in (0, 1):
        second.sibling_own(half)
        for which in range(3):
            second.sibling_other(which, half)
    for copy in shared:
        copy.wait_recv()

    heard(3)

    zs = nz // TP

    def make_term(turn):
        owner = lax.rem(lax.div(z, zs) + turn, TP)
        rows = columns[owner].reshape(zs * 64, DP * PATCHES)
        result = jnp.dot(rows, dkv[...], preferred_element_type=F32)
        term[pl.ds(owner * zs, zs)] = result.reshape(zs, 64, KVC)

    lanes = ring_lanes(nz)
    height = 64 // PARTS

    def target(lane, step):
        way, base, size, _ = lane
        away = base + size - step
        return lax.rem((z + away, z + nz - away)[way], nz)

    def ring_copy(lane, step, piece):
        way, _, size, first = lane
        rows = pl.ds(piece * height, height)
        to = target(lane, step) if step == size - 1 else (z_next, z_prev)[way]
        place = first + step
        return remote(
            ring_out.at[place, rows, :],
            ring_in.at[place, rows, :],
            ring_send.at[place * PARTS + piece],
            ring_recv.at[place * PARTS + piece],
            seq=to,
        )

    def ring_step(lane, step):
        place = lane[3] + step
        for piece in range(PARTS):
            rows = pl.ds(piece * height, height)
            total = term[target(lane, step), rows, :]
            if step:
                ring_copy(lane, step - 1, piece).wait_recv()
                total += ring_in[place - 1, rows, :].astype(F32)
            ring_out[place, rows, :] = total.astype(BF16)
            ring_copy(lane, step, piece).start()

    for turn in (4, 5):
        make_term(turn)
    for lane in lanes[:2]:
        ring_step(lane, 0)
    for turn in (3, 2, 6):
        make_term(turn)
    for lane in lanes[2:4]:
        ring_step(lane, 0)
    for turn in (1, 7, 0):
        make_term(turn)
    for lane in lanes[4:]:
        ring_step(lane, 0)
    for step in range(1, max(lane[2] for lane in lanes)):
        for lane in lanes:
            if step < lane[2]:
                ring_step(lane, step)

    total = term[z]
    for lane in lanes[::-1]:
        for piece in range(PARTS):
            ring_copy(lane, lane[2] - 1, piece).wait_recv()
        total += ring_in[lane[3] + lane[2] - 1].astype(F32)
    quarter[dp] = total
    last = []
    for steps in range(1, DP):
        copy = remote(
            quarter.at[dp],
            quarter.at[dp],
            last_send.at[steps - 1],
            last_recv.at[steps - 1],
            dp=lax.rem(dp + steps, DP),
        )
        copy.start()
        last.append(copy)

    gather.finish()
    second.finish()
    for copy in cross + halo + chain + shared:
        copy.wait_send()

    for lane in lanes:
        for step in range(lane[2]):
            for piece in range(PARTS):
                ring_copy(lane, step, piece).wait_send()
    out_att.wait()
    out_dq.wait()
    for steps in range(1, DP):
        source = lax.rem(dp + DP - steps, DP)
        remote(
            quarter.at[source],
            quarter.at[source],
            last_send.at[steps - 1],
            last_recv.at[steps - 1],
            dp=source,
        ).wait_recv()
    for copy in last:
        copy.wait_send()
    weight_out[...] = quarter[...].reshape(DP * 64, KVC)


def local(nz, queries, images, kv_weight, gate, cotangent, span_first, span_last):
    zs = nz // TP
    any_space = pl.BlockSpec(memory_space=pltpu.HBM)
    vmem = pl.BlockSpec(memory_space=pltpu.VMEM)
    smem = pl.BlockSpec(memory_space=pltpu.SMEM)
    dma = pltpu.SemaphoreType.DMA
    rows = REACH * PATCHES
    low = lambda *shape: pltpu.VMEM(shape, BF16)
    wide = lambda *shape: pltpu.VMEM(shape, F32)
    return pl.pallas_call(
        functools.partial(kernel, nz),
        out_shape=(
            jax.ShapeDtypeStruct(queries.shape, BF16),
            jax.ShapeDtypeStruct(queries.shape, BF16),
            jax.ShapeDtypeStruct((DP * 64, KVC), F32),
        ),
        in_specs=[any_space, any_space, any_space, smem, any_space, smem, smem],
        out_specs=(any_space, any_space, vmem),
        scratch_shapes=[
            low(TOKENS, SHARD),
            low(TOKENS, SHARD),
            low(TP * SHARD, KVC),
            low(TP, PATCHES, SHARD),
            wide(PATCHES, KVC),
            low(zs, DP, 64, PATCHES),
            low(TP, zs, 64, DP * PATCHES),
            low(HEAD_SIZE, SHARD),
            low(TOKENS, SHARD),
            low(HEAD_SIZE, SHARD),
            low(rows, HEAD_SIZE),
            low(rows, HEAD_SIZE),
            wide(HEADS, TOKENS, rows),
            wide(HEADS, TOKENS, rows),
            low(HEADS * TOKENS, rows),
            low(HEADS * TOKENS, rows),
            low(TOKENS, SHARD),
            low(TOKENS, SHARD),
            wide(REACH, 2, PATCHES, HEAD_SIZE),
            low(REACH - 1, 2, PATCHES, HEAD_SIZE),
            low(REACH - 1, 2, PATCHES, HEAD_SIZE),
            low(DP * PATCHES, KVC),
            wide(nz, 64, KVC),
            low(nz - 1, 64, KVC),
            low(nz - 1, 64, KVC),
            wide(DP, 64, KVC),
            dma((7,)),
            dma((GATHER_COPIES,)),
            dma((GATHER_COPIES,)),
            dma((GATHER_COPIES,)),
            dma((GATHER_COPIES,)),
            dma((DP - 1,)),
            dma((DP - 1,)),
            dma((2 * (REACH - 1),)),
            dma((2 * (REACH - 1),)),
            dma((2 * (REACH - 1),)),
            dma((2 * (REACH - 1),)),
            dma((DP - 1,)),
            dma((DP - 1,)),
            dma(((nz - 1) * PARTS,)),
            dma(((nz - 1) * PARTS,)),
            dma((DP - 1,)),
            dma((DP - 1,)),
            pltpu.SemaphoreType.REGULAR((2 * len(GREETINGS),)),
        ],
        compiler_params=pltpu.CompilerParams(
            collective_id=0, has_side_effects=True, vmem_limit_bytes=67043328
        ),
        name="cross_attention",
    )(queries, images, kv_weight, gate, cotangent, span_first, span_last)


def solution(mesh):
    return jax.shard_map(
        functools.partial(local, mesh.shape["seq"]),
        mesh=mesh,
        in_specs=(
            P("dp", "seq", "tp"),
            P("dp", "seq", None, "tp"),
            P(None, "tp"),
            P(),
            P("dp", "seq", "tp"),
            P("dp", "seq"),
            P("dp", "seq"),
        ),
        out_specs=(P("dp", "seq", "tp"), P("dp", "seq", "tp"), P("seq", "tp")),
        check_vma=False,
    )
```

```python
import functools

import jax
import jax.numpy as jnp
from jax import lax
from jax.experimental import pallas as pl
from jax.experimental.pallas import tpu as pltpu
from jax.sharding import PartitionSpec as P

HEADS = 8
HEAD_SIZE = 128
TOKENS = 128
PATCHES = 128
REACH = 4
TP = 8
DP = 4
SHARD = 1024
HALF = SHARD // 2
KVC = 2 * HEAD_SIZE
SCALE = HEAD_SIZE ** (-0.5)
GATHER_COPIES = 14
GREETINGS = (1, 2, 4, 4)
STRETCHES = ((9, 7), (8, 7))
PARTS = 2

BF16 = jnp.bfloat16
F32 = jnp.float32


def remote(src, dst, send_sem, recv_sem, **where):
    return pltpu.make_async_remote_copy(
        src_ref=src,
        dst_ref=dst,
        send_sem=send_sem,
        recv_sem=recv_sem,
        device_id=where,
        device_id_type=pl.DeviceIdType.MESH,
    )


def ring_lanes(nz):
    lanes, slot = [], 0
    for way in range(2):
        base = 0
        for size in STRETCHES[way]:
            lanes.append((way, base, size, slot))
            base, slot = base + size, slot + size
        assert base == nz // 2 - way
    return sorted(lanes, key=lambda lane: -lane[1] - lane[2])


class RowGather:
    def __init__(self, own, slot, send_sems, recv_sems):
        tp = lax.axis_index("tp")
        self.tp = tp
        self.right, self.left = lax.rem(tp + 2, TP), lax.rem(tp + TP - 2, TP)
        self.opposite = lax.rem(tp + 4, TP)
        self.sibling = tp + 1 - 2 * lax.rem(tp, 2)
        self.own, self.slot = own, slot
        self.send_sems, self.recv_sems = send_sems, recv_sems
        self.started = []

    def _copy(self, index, src, dst, target):
        return remote(src, dst, self.send_sems.at[index], self.recv_sems.at[index], tp=target)

    def _start(self, index, src, owner, half, target):
        copy = self._copy(index, src, self.slot(owner, half), target)
        copy.start()
        self.started.append(copy)

    def _arrived(self, index, owner, half):
        ref = self.slot(owner, half)
        self._copy(index, ref, ref, self.right).wait_recv()

    def send_own(self):
        for half in (0, 1):
            self._start(half, self.own(half), self.tp, half, self.right)
            self._start(3 - half, self.own(1 - half), self.tp, 1 - half, self.left)
        for half in (0, 1):
            self._start(6 + half, self.own(half), self.tp, half, self.sibling)

    def sibling_own(self, half):
        self._arrived(6 + half, self.sibling, half)
        return self.sibling, half

    def from_left(self, half):
        self._arrived(half, self.left, half)
        ref = self.slot(self.left, half)
        if half == 0:
            self._start(4, ref, self.left, half, self.right)
        self._start(8 + half, ref, self.left, half, self.sibling)
        return self.left, half

    def from_right(self, half):
        self._arrived(2 + half, self.right, half)
        ref = self.slot(self.right, half)
        if half == 1:
            self._start(5, ref, self.right, half, self.left)
        self._start(10 + half, ref, self.right, half, self.sibling)
        return self.right, half

    def from_opposite(self, half):
        self._arrived(4 + half, self.opposite, half)
        self._start(12 + half, self.slot(self.opposite, half), self.opposite, half, self.sibling)
        return self.opposite, half

    def sibling_other(self, which, half):
        owner = lax.rem(self.sibling + (TP - 2, 2, 4)[which], TP)
        self._arrived(8 + 2 * which + half, owner, half)
        return owner, half

    def finish(self):
        for copy in self.started:
            copy.wait_send()


def kernel(
    nz,
    queries,
    features,
    kv_weight,
    gate,
    cotangent,
    span_first,
    span_last,
    attended_out,
    query_grad_out,
    weight_out,
    q_buf,
    cot_buf,
    w_buf,
    gathered,
    proj,
    transposed,
    columns,
    q_t,
    dc_buf,
    dc_t,
    keys,
    values,
    scores,
    d_probs,
    p_buf,
    ds_buf,
    att_buf,
    dq_buf,
    part,
    chain_out,
    chain_in,
    dkv,
    term,
    ring_out,
    ring_in,
    quarter,
    local_sems,
    feat_send,
    feat_recv,
    col_send,
    col_recv,
    cross_send,
    cross_recv,
    kv_send,
    kv_recv,
    chain_send,
    chain_recv,
    dkv_send,
    dkv_recv,
    ring_send,
    ring_recv,
    last_send,
    last_recv,
    greeted,
):
    z, tp, dp = lax.axis_index("seq"), lax.axis_index("tp"), lax.axis_index("dp")
    z_next, z_prev = lax.rem(z + 1, nz), lax.rem(z + nz - 1, nz)

    in_q = pltpu.make_async_copy(queries.at[0], q_buf, local_sems.at[0])
    in_cot = pltpu.make_async_copy(cotangent.at[0], cot_buf, local_sems.at[1])
    in_w = pltpu.make_async_copy(kv_weight, w_buf, local_sems.at[2])
    in_f = pltpu.make_async_copy(features.at[0, 0], gathered.at[lax.axis_index('tp')], local_sems.at[6])
    in_f.start()
    in_q.start()
    in_cot.start()
    in_w.start()

    gather = RowGather(
        lambda half: features.at[0, 0, :, pl.ds(half * HALF, HALF)],
        lambda owner, half: gathered.at[owner, :, pl.ds(half * HALF, HALF)],
        feat_send,
        feat_recv,
    )
    barrier = pltpu.get_barrier_semaphore()
    mesh_id = pl.DeviceIdType.MESH
    for other in (gather.right, gather.left, gather.sibling):
        pl.semaphore_signal(barrier, inc=1, device_id={"tp": other}, device_id_type=mesh_id)
    for steps in range(1, DP):
        other = lax.rem(dp + steps, DP)
        pl.semaphore_signal(barrier, inc=1, device_id={"dp": other}, device_id_type=mesh_id)
    for other in (z_next, z_prev):
        pl.semaphore_signal(barrier, inc=1, device_id={"seq": other}, device_id_type=mesh_id)
    pl.semaphore_wait(barrier, 8)

    def greet(turn):
        for way in range(2):
            step = GREETINGS[turn]
            other = lax.rem((z + step, z + nz - step)[way], nz)
            pl.semaphore_signal(greeted.at[turn * 2 + way], inc=1, device_id={"seq": other}, device_id_type=mesh_id)

    def heard(turn):
        for way in range(2):
            pl.semaphore_wait(greeted.at[turn * 2 + way], 1)

    gather.send_own()
    greet(0)
    in_f.wait()

    for block in range(SHARD // 128):
        tile = gathered[tp, :, block * 128 : (block + 1) * 128].astype(F32)
        flipped = jnp.transpose(tile).astype(BF16)
        for piece in range(2):
            place = block * 2 + piece
            transposed[place // 4, place % 4] = flipped[piece * 64 : (piece + 1) * 64]
    own_quarter = pltpu.make_async_copy(
        transposed.at[:, dp], columns.at[tp, :, :, pl.ds(0, 128)], local_sems.at[3]
    )
    own_quarter.start()
    cross = []
    for steps in range(1, DP):
        to = lax.rem(dp + steps, DP)
        copy = remote(
            transposed.at[:, to],
            columns.at[tp, :, :, pl.ds(steps * 128, 128)],
            cross_send.at[steps - 1],
            cross_recv.at[steps - 1],
            dp=to,
        )
        copy.start()
        cross.append(copy)

    in_w.wait()

    def project(owner, half):
        rows = pl.ds(pl.multiple_of(owner * SHARD + half * HALF, HALF), HALF)
        block = gathered[owner, :, half * HALF : (half + 1) * HALF]
        return jnp.dot(block, w_buf[rows, :], preferred_element_type=F32)

    proj[...] = project(tp, 0) + project(tp, 1)
    for half in (0, 1):
        proj[...] += project(*gather.sibling_own(half))

    in_q.wait()
    in_cot.wait()
    gate_tanh = jnp.tanh(jnp.full((8, 128), gate[0], F32))[:1]

    def prepare(head, _):
        lanes = pl.ds(pl.multiple_of(head * HEAD_SIZE, HEAD_SIZE), HEAD_SIZE)
        low = (gate_tanh * cot_buf[:, lanes].astype(F32)).astype(BF16)
        dc_buf[:, lanes] = low
        dc_t[:, lanes] = jnp.transpose(low.astype(F32)).astype(BF16)
        q_t[:, lanes] = jnp.transpose(q_buf[:, lanes].astype(F32)).astype(BF16)
        return 0

    lax.fori_loop(0, HEADS, prepare, 0, unroll=True)
    heard(0)
    greet(1)

    arrived = [gather.from_left(0), gather.from_right(1)]
    for owner, half in arrived:
        proj[...] += project(owner, half)
    arrived = [gather.from_left(1), gather.from_right(0)]
    for owner, half in arrived:
        proj[...] += project(owner, half)
    for which, half in ((0, 0), (1, 1), (0, 1), (1, 0)):
        proj[...] += project(*gather.sibling_other(which, half))
    arrived = [gather.from_opposite(0), gather.from_opposite(1)]
    for owner, half in arrived:
        proj[...] += project(owner, half)
    for half in (0, 1):
        proj[...] += project(*gather.sibling_other(2, half))

    keys[pl.ds(0, PATCHES), :] = proj[:, :HEAD_SIZE].astype(BF16)
    values[pl.ds(0, PATCHES), :] = proj[:, HEAD_SIZE:].astype(BF16)

    z_after, z_before = lax.rem(z + 2, nz), lax.rem(z + nz - 2, nz)
    halo = []

    def pass_on(source, offset, to):
        for side, rows in enumerate((keys, values)):
            copy = remote(
                rows.at[pl.ds(source * PATCHES, PATCHES), :],
                rows.at[pl.ds(offset * PATCHES, PATCHES), :],
                kv_send.at[offset * 2 - 2 + side],
                kv_recv.at[offset * 2 - 2 + side],
                seq=to,
            )
            copy.start()
            halo.append(copy)

    pass_on(0, 2, z_after)
    pass_on(0, 1, z_next)

    own_quarter.wait()
    for copy in cross:
        copy.wait_recv()
    second = RowGather(
        lambda half: columns.at[tp, pl.ds(half * 2, 2)],
        lambda owner, half: columns.at[owner, pl.ds(half * 2, 2)],
        col_send,
        col_recv,
    )
    second.send_own()

    def score(offset):
        rows = pl.ds(offset * PATCHES, PATCHES)
        nt = (((1,), (1,)), ((), ()))

        def one(head, _):
            lanes = pl.ds(pl.multiple_of(head * HEAD_SIZE, HEAD_SIZE), HEAD_SIZE)
            scores[head, :, rows] = lax.dot_general(
                q_buf[:, lanes], keys[rows, :], nt, preferred_element_type=F32
            )
            d_probs[head, :, rows] = lax.dot_general(
                dc_buf[:, lanes], values[rows, :], nt, preferred_element_type=F32
            )
            return 0

        lax.fori_loop(0, HEADS, one, 0, unroll=True)

    heard(1)
    greet(2)
    score(0)
    for copy in halo[:2]:
        copy.wait_recv()
    pass_on(2, 3, z_next)
    score(2)
    for copy in halo[2:4]:
        copy.wait_recv()
    score(1)
    for copy in halo[4:]:
        copy.wait_recv()
    score(3)

    second.from_left(0)
    second.from_right(1)
    second.from_left(1)
    second.from_right(0)

    lane = lax.broadcasted_iota(jnp.int32, (1, REACH * PATCHES), 1)
    image = z - lax.div(lane, PATCHES)
    is_live = (image >= span_first[0, 0]) & (image <= span_last[0, 0])
    bias = jnp.where(is_live, 0.0, -jnp.inf).astype(F32)

    def attend(head, _):
        lanes = pl.ds(pl.multiple_of(head * HEAD_SIZE, HEAD_SIZE), HEAD_SIZE)
        rows = pl.ds(pl.multiple_of(head * TOKENS, TOKENS), TOKENS)
        logits = scores[head] * SCALE + bias
        exponent = jnp.exp(logits - jnp.max(logits, axis=1, keepdims=True))
        prob = exponent * (1.0 / jnp.sum(exponent, axis=1, keepdims=True))
        prob_low = prob.astype(BF16)
        context = jnp.dot(prob_low, values[...], preferred_element_type=F32)
        att_buf[:, lanes] = (gate_tanh * context).astype(BF16)
        delta = jnp.sum(dc_buf[:, lanes].astype(F32) * context, axis=1, keepdims=True)
        d_score = (prob * (d_probs[head] - delta) * SCALE).astype(BF16)
        dq_buf[:, lanes] = jnp.dot(d_score, keys[...], preferred_element_type=F32).astype(BF16)
        p_buf[rows, :] = prob_low
        ds_buf[rows, :] = d_score
        return 0

    heard(2)
    greet(3)
    lax.fori_loop(0, HEADS, attend, 0, unroll=True)
    out_att = pltpu.make_async_copy(att_buf, attended_out.at[0], local_sems.at[4])
    out_dq = pltpu.make_async_copy(dq_buf, query_grad_out.at[0], local_sems.at[5])
    out_att.start()
    out_dq.start()

    def partial_gradients(pair):
        window = pl.ds(pair * 2 * PATCHES, 2 * PATCHES)
        for side, (left_ref, right_ref) in enumerate(((q_t, ds_buf), (dc_t, p_buf))):
            both = jnp.dot(left_ref[...], right_ref[:, window], preferred_element_type=F32)
            for index in range(2):
                tile = both[:, index * PATCHES : (index + 1) * PATCHES]
                part[pair * 2 + index, side] = jnp.transpose(tile)

    chain = []

    def hand_back(step, to):
        for side in range(2):
            copy = remote(
                chain_out.at[step, side],
                chain_in.at[step, side],
                chain_send.at[step * 2 + side],
                chain_recv.at[step * 2 + side],
                seq=to,
            )
            copy.start()
            chain.append(copy)

    partial_gradients(1)
    chain_out[0] = part[3].astype(BF16)
    hand_back(0, z_prev)
    partial_gradients(0)
    chain_out[2] = part[1].astype(BF16)
    hand_back(2, z_prev)
    second.from_opposite(0)
    second.from_opposite(1)
    for copy in chain[:2]:
        copy.wait_recv()
    chain_out[1] = (part[2] + chain_in[0].astype(F32)).astype(BF16)
    hand_back(1, z_before)
    for copy in chain[2:]:
        copy.wait_recv()
    total = part[0] + chain_in[2].astype(F32) + chain_in[1].astype(F32)
    dkv[pl.ds(0, PATCHES), pl.ds(0, HEAD_SIZE)] = total[0].astype(BF16)
    dkv[pl.ds(0, PATCHES), pl.ds(HEAD_SIZE, HEAD_SIZE)] = total[1].astype(BF16)

    shared = []
    for steps in range(1, DP):
        copy = remote(
            dkv.at[pl.ds(0, PATCHES), :],
            dkv.at[pl.ds(steps * PATCHES, PATCHES), :],
            dkv_send.at[steps - 1],
            dkv_recv.at[steps - 1],
            dp=lax.rem(dp + steps, DP),
        )
        copy.start()
        shared.append(copy)
    for half in (0, 1):
        second.sibling_own(half)
        for which in range(3):
            second.sibling_other(which, half)
    for copy in shared:
        copy.wait_recv()

    heard(3)

    zs = nz // TP

    def make_term(turn):
        owner = lax.rem(lax.div(z, zs) + turn, TP)
        rows = columns[owner].reshape(zs * 64, DP * PATCHES)
        result = jnp.dot(rows, dkv[...], preferred_element_type=F32)
        term[pl.ds(owner * zs, zs)] = result.reshape(zs, 64, KVC)

    lanes = ring_lanes(nz)
    height = 64 // PARTS

    def target(lane, step):
        way, base, size, _ = lane
        away = base + size - step
        return lax.rem((z + away, z + nz - away)[way], nz)

    def ring_copy(lane, step, piece):
        way, _, size, first = lane
        rows = pl.ds(piece * height, height)
        to = target(lane, step) if step == size - 1 else (z_next, z_prev)[way]
        place = first + step
        return remote(
            ring_out.at[place, rows, :],
            ring_in.at[place, rows, :],
            ring_send.at[place * PARTS + piece],
            ring_recv.at[place * PARTS + piece],
            seq=to,
        )

    def ring_step(lane, step):
        place = lane[3] + step
        for piece in range(PARTS):
            rows = pl.ds(piece * height, height)
            total = term[target(lane, step), rows, :]
            if step:
                ring_copy(lane, step - 1, piece).wait_recv()
                total += ring_in[place - 1, rows, :].astype(F32)
            ring_out[place, rows, :] = total.astype(BF16)
            ring_copy(lane, step, piece).start()

    for turn in (4, 5):
        make_term(turn)
    for lane in lanes[:2]:
        ring_step(lane, 0)
    for turn in (3, 2, 6):
        make_term(turn)
    for lane in lanes[2:4]:
        ring_step(lane, 0)
    for turn in (1, 7, 0):
        make_term(turn)
    for lane in lanes[4:]:
        ring_step(lane, 0)
    for step in range(1, max(lane[2] for lane in lanes)):
        for lane in lanes:
            if step < lane[2]:
                ring_step(lane, step)

    total = term[z]
    for lane in lanes[::-1]:
        for piece in range(PARTS):
            ring_copy(lane, lane[2] - 1, piece).wait_recv()
        total += ring_in[lane[3] + lane[2] - 1].astype(F32)
    quarter[dp] = total.astype(BF16)
    last = []
    for steps in range(1, DP):
        copy = remote(
            quarter.at[dp],
            quarter.at[dp],
            last_send.at[steps - 1],
            last_recv.at[steps - 1],
            dp=lax.rem(dp + steps, DP),
        )
        copy.start()
        last.append(copy)

    gather.finish()
    second.finish()
    for copy in cross + halo + chain + shared:
        copy.wait_send()

    for lane in lanes:
        for step in range(lane[2]):
            for piece in range(PARTS):
                ring_copy(lane, step, piece).wait_send()
    out_att.wait()
    out_dq.wait()
    for steps in range(1, DP):
        source = lax.rem(dp + DP - steps, DP)
        remote(
            quarter.at[source],
            quarter.at[source],
            last_send.at[steps - 1],
            last_recv.at[steps - 1],
            dp=source,
        ).wait_recv()
    for copy in last:
        copy.wait_send()
    weight_out[...] = quarter[...].reshape(DP * 64, KVC).astype(F32)


def local(nz, queries, images, kv_weight, gate, cotangent, span_first, span_last):
    zs = nz // TP
    any_space = pl.BlockSpec(memory_space=pltpu.HBM)
    vmem = pl.BlockSpec(memory_space=pltpu.VMEM)
    smem = pl.BlockSpec(memory_space=pltpu.SMEM)
    dma = pltpu.SemaphoreType.DMA
    rows = REACH * PATCHES
    low = lambda *shape: pltpu.VMEM(shape, BF16)
    wide = lambda *shape: pltpu.VMEM(shape, F32)
    return pl.pallas_call(
        functools.partial(kernel, nz),
        out_shape=(
            jax.ShapeDtypeStruct(queries.shape, BF16),
            jax.ShapeDtypeStruct(queries.shape, BF16),
            jax.ShapeDtypeStruct((DP * 64, KVC), F32),
        ),
        in_specs=[any_space, any_space, any_space, smem, any_space, smem, smem],
        out_specs=(any_space, any_space, vmem),
        scratch_shapes=[
            low(TOKENS, SHARD),
            low(TOKENS, SHARD),
            low(TP * SHARD, KVC),
            low(TP, PATCHES, SHARD),
            wide(PATCHES, KVC),
            low(zs, DP, 64, PATCHES),
            low(TP, zs, 64, DP * PATCHES),
            low(HEAD_SIZE, SHARD),
            low(TOKENS, SHARD),
            low(HEAD_SIZE, SHARD),
            low(rows, HEAD_SIZE),
            low(rows, HEAD_SIZE),
            wide(HEADS, TOKENS, rows),
            wide(HEADS, TOKENS, rows),
            low(HEADS * TOKENS, rows),
            low(HEADS * TOKENS, rows),
            low(TOKENS, SHARD),
            low(TOKENS, SHARD),
            wide(REACH, 2, PATCHES, HEAD_SIZE),
            low(REACH - 1, 2, PATCHES, HEAD_SIZE),
            low(REACH - 1, 2, PATCHES, HEAD_SIZE),
            low(DP * PATCHES, KVC),
            wide(nz, 64, KVC),
            low(nz - 1, 64, KVC),
            low(nz - 1, 64, KVC),
            low(DP, 64, KVC),
            dma((7,)),
            dma((GATHER_COPIES,)),
            dma((GATHER_COPIES,)),
            dma((GATHER_COPIES,)),
            dma((GATHER_COPIES,)),
            dma((DP - 1,)),
            dma((DP - 1,)),
            dma((2 * (REACH - 1),)),
            dma((2 * (REACH - 1),)),
            dma((2 * (REACH - 1),)),
            dma((2 * (REACH - 1),)),
            dma((DP - 1,)),
            dma((DP - 1,)),
            dma(((nz - 1) * PARTS,)),
            dma(((nz - 1) * PARTS,)),
            dma((DP - 1,)),
            dma((DP - 1,)),
            pltpu.SemaphoreType.REGULAR((2 * len(GREETINGS),)),
        ],
        compiler_params=pltpu.CompilerParams(
            collective_id=0, has_side_effects=True, vmem_limit_bytes=67043328
        ),
        name="cross_attention",
    )(queries, images, kv_weight, gate, cotangent, span_first, span_last)


def solution(mesh):
    return jax.shard_map(
        functools.partial(local, mesh.shape["seq"]),
        mesh=mesh,
        in_specs=(
            P("dp", "seq", "tp"),
            P("dp", "seq", None, "tp"),
            P(None, "tp"),
            P(),
            P("dp", "seq", "tp"),
            P("dp", "seq"),
            P("dp", "seq"),
        ),
        out_specs=(P("dp", "seq", "tp"), P("dp", "seq", "tp"), P("seq", "tp")),
        check_vma=False,
    )
```

```python
import functools

import jax
import jax.numpy as jnp
from jax import lax
from jax.experimental import pallas as pl
from jax.experimental.pallas import tpu as pltpu
from jax.sharding import PartitionSpec as P

HEADS = 8
HEAD_SIZE = 128
TOKENS = 128
PATCHES = 128
REACH = 4
TP = 8
DP = 4
SHARD = 1024
HALF = SHARD // 2
KVC = 2 * HEAD_SIZE
SCALE = HEAD_SIZE ** (-0.5)
GATHER_COPIES = 14
GREETINGS = (1, 2, 4, 4)
STRETCHES = ((9, 7), (8, 7))
PARTS = 2

BF16 = jnp.bfloat16
F32 = jnp.float32


def remote(src, dst, send_sem, recv_sem, **where):
    return pltpu.make_async_remote_copy(
        src_ref=src,
        dst_ref=dst,
        send_sem=send_sem,
        recv_sem=recv_sem,
        device_id=where,
        device_id_type=pl.DeviceIdType.MESH,
    )


def ring_lanes(nz):
    lanes, slot = [], 0
    for way in range(2):
        base = 0
        for size in STRETCHES[way]:
            lanes.append((way, base, size, slot))
            base, slot = base + size, slot + size
        assert base == nz // 2 - way
    return sorted(lanes, key=lambda lane: -lane[1] - lane[2])


class RowGather:
    def __init__(self, own, slot, send_sems, recv_sems):
        tp = lax.axis_index("tp")
        self.tp = tp
        self.right, self.left = lax.rem(tp + 2, TP), lax.rem(tp + TP - 2, TP)
        self.opposite = lax.rem(tp + 4, TP)
        self.sibling = tp + 1 - 2 * lax.rem(tp, 2)
        self.own, self.slot = own, slot
        self.send_sems, self.recv_sems = send_sems, recv_sems
        self.started = []

    def _copy(self, index, src, dst, target):
        return remote(src, dst, self.send_sems.at[index], self.recv_sems.at[index], tp=target)

    def _start(self, index, src, owner, half, target):
        copy = self._copy(index, src, self.slot(owner, half), target)
        copy.start()
        self.started.append(copy)

    def _arrived(self, index, owner, half):
        ref = self.slot(owner, half)
        self._copy(index, ref, ref, self.right).wait_recv()

    def send_own(self):
        for half in (0, 1):
            self._start(half, self.own(half), self.tp, half, self.right)
            self._start(3 - half, self.own(1 - half), self.tp, 1 - half, self.left)
        for half in (0, 1):
            self._start(6 + half, self.own(half), self.tp, half, self.sibling)

    def sibling_own(self, half):
        self._arrived(6 + half, self.sibling, half)
        return self.sibling, half

    def from_left(self, half):
        self._arrived(half, self.left, half)
        ref = self.slot(self.left, half)
        if half == 0:
            self._start(4, ref, self.left, half, self.right)
        self._start(8 + half, ref, self.left, half, self.sibling)
        return self.left, half

    def from_right(self, half):
        self._arrived(2 + half, self.right, half)
        ref = self.slot(self.right, half)
        if half == 1:
            self._start(5, ref, self.right, half, self.left)
        self._start(10 + half, ref, self.right, half, self.sibling)
        return self.right, half

    def from_opposite(self, half):
        self._arrived(4 + half, self.opposite, half)
        self._start(12 + half, self.slot(self.opposite, half), self.opposite, half, self.sibling)
        return self.opposite, half

    def sibling_other(self, which, half):
        owner = lax.rem(self.sibling + (TP - 2, 2, 4)[which], TP)
        self._arrived(8 + 2 * which + half, owner, half)
        return owner, half

    def finish(self):
        for copy in self.started:
            copy.wait_send()


def kernel(
    nz,
    queries,
    features,
    kv_weight,
    gate,
    cotangent,
    span_first,
    span_last,
    attended_out,
    query_grad_out,
    weight_out,
    q_buf,
    cot_buf,
    w_buf,
    gathered,
    proj,
    transposed,
    columns,
    q_t,
    dc_buf,
    dc_t,
    keys,
    values,
    scores,
    d_probs,
    p_buf,
    ds_buf,
    att_buf,
    dq_buf,
    part,
    chain_out,
    chain_in,
    dkv,
    term,
    ring_out,
    ring_in,
    quarter,
    local_sems,
    feat_send,
    feat_recv,
    col_send,
    col_recv,
    cross_send,
    cross_recv,
    kv_send,
    kv_recv,
    chain_send,
    chain_recv,
    dkv_send,
    dkv_recv,
    ring_send,
    ring_recv,
    last_send,
    last_recv,
    greeted,
):
    z, tp, dp = lax.axis_index("seq"), lax.axis_index("tp"), lax.axis_index("dp")
    z_next, z_prev = lax.rem(z + 1, nz), lax.rem(z + nz - 1, nz)

    in_q = pltpu.make_async_copy(queries.at[0], q_buf, local_sems.at[0])
    in_cot = pltpu.make_async_copy(cotangent.at[0], cot_buf, local_sems.at[1])
    in_w = pltpu.make_async_copy(kv_weight, w_buf, local_sems.at[2])
    in_f = pltpu.make_async_copy(features.at[0, 0], gathered.at[lax.axis_index('tp')], local_sems.at[6])
    in_f.start()
    in_q.start()
    in_cot.start()
    in_w.start()

    gather = RowGather(
        lambda half: features.at[0, 0, :, pl.ds(half * HALF, HALF)],
        lambda owner, half: gathered.at[owner, :, pl.ds(half * HALF, HALF)],
        feat_send,
        feat_recv,
    )
    barrier = pltpu.get_barrier_semaphore()
    mesh_id = pl.DeviceIdType.MESH
    for other in (gather.right, gather.left, gather.sibling):
        pl.semaphore_signal(barrier, inc=1, device_id={"tp": other}, device_id_type=mesh_id)
    for steps in range(1, DP):
        other = lax.rem(dp + steps, DP)
        pl.semaphore_signal(barrier, inc=1, device_id={"dp": other}, device_id_type=mesh_id)
    for other in (z_next, z_prev):
        pl.semaphore_signal(barrier, inc=1, device_id={"seq": other}, device_id_type=mesh_id)
    pl.semaphore_wait(barrier, 8)

    def greet(turn):
        for way in range(2):
            step = GREETINGS[turn]
            other = lax.rem((z + step, z + nz - step)[way], nz)
            pl.semaphore_signal(greeted.at[turn * 2 + way], inc=1, device_id={"seq": other}, device_id_type=mesh_id)

    def heard(turn):
        for way in range(2):
            pl.semaphore_wait(greeted.at[turn * 2 + way], 1)

    gather.send_own()
    greet(0)
    in_f.wait()

    for block in range(SHARD // 128):
        tile = gathered[tp, :, block * 128 : (block + 1) * 128].astype(F32)
        flipped = jnp.transpose(tile).astype(BF16)
        for piece in range(2):
            place = block * 2 + piece
            transposed[place // 4, place % 4] = flipped[piece * 64 : (piece + 1) * 64]
    own_quarter = pltpu.make_async_copy(
        transposed.at[:, dp], columns.at[tp, :, :, pl.ds(0, 128)], local_sems.at[3]
    )
    own_quarter.start()
    cross = []
    for steps in range(1, DP):
        to = lax.rem(dp + steps, DP)
        copy = remote(
            transposed.at[:, to],
            columns.at[tp, :, :, pl.ds(steps * 128, 128)],
            cross_send.at[steps - 1],
            cross_recv.at[steps - 1],
            dp=to,
        )
        copy.start()
        cross.append(copy)

    in_w.wait()

    def project(owner, half):
        rows = pl.ds(pl.multiple_of(owner * SHARD + half * HALF, HALF), HALF)
        block = gathered[owner, :, half * HALF : (half + 1) * HALF]
        return jnp.dot(block, w_buf[rows, :], preferred_element_type=F32)

    proj[...] = project(tp, 0) + project(tp, 1)
    for half in (0, 1):
        proj[...] += project(*gather.sibling_own(half))

    in_q.wait()
    in_cot.wait()
    gate_tanh = jnp.tanh(jnp.full((8, 128), gate[0], F32))[:1]

    def prepare(head, _):
        lanes = pl.ds(pl.multiple_of(head * HEAD_SIZE, HEAD_SIZE), HEAD_SIZE)
        low = (gate_tanh * cot_buf[:, lanes].astype(F32)).astype(BF16)
        dc_buf[:, lanes] = low
        dc_t[:, lanes] = jnp.transpose(low.astype(F32)).astype(BF16)
        q_t[:, lanes] = jnp.transpose(q_buf[:, lanes].astype(F32)).astype(BF16)
        return 0

    lax.fori_loop(0, HEADS, prepare, 0, unroll=True)
    heard(0)
    greet(1)

    arrived = [gather.from_left(0), gather.from_right(1)]
    for owner, half in arrived:
        proj[...] += project(owner, half)
    arrived = [gather.from_left(1), gather.from_right(0)]
    for owner, half in arrived:
        proj[...] += project(owner, half)
    for which, half in ((0, 0), (1, 1), (0, 1), (1, 0)):
        proj[...] += project(*gather.sibling_other(which, half))
    arrived = [gather.from_opposite(0), gather.from_opposite(1)]
    for owner, half in arrived:
        proj[...] += project(owner, half)
    for half in (0, 1):
        proj[...] += project(*gather.sibling_other(2, half))

    keys[pl.ds(0, PATCHES), :] = proj[:, :HEAD_SIZE].astype(BF16)
    values[pl.ds(0, PATCHES), :] = proj[:, HEAD_SIZE:].astype(BF16)

    z_after, z_before = lax.rem(z + 2, nz), lax.rem(z + nz - 2, nz)
    halo = []

    def pass_on(source, offset, to):
        for side, rows in enumerate((keys, values)):
            copy = remote(
                rows.at[pl.ds(source * PATCHES, PATCHES), :],
                rows.at[pl.ds(offset * PATCHES, PATCHES), :],
                kv_send.at[offset * 2 - 2 + side],
                kv_recv.at[offset * 2 - 2 + side],
                seq=to,
            )
            copy.start()
            halo.append(copy)

    pass_on(0, 2, z_after)
    pass_on(0, 1, z_next)

    own_quarter.wait()
    for copy in cross:
        copy.wait_recv()
    second = RowGather(
        lambda half: columns.at[tp, pl.ds(half * 2, 2)],
        lambda owner, half: columns.at[owner, pl.ds(half * 2, 2)],
        col_send,
        col_recv,
    )
    second.send_own()

    def score(offset):
        rows = pl.ds(offset * PATCHES, PATCHES)
        nt = (((1,), (1,)), ((), ()))

        def one(head, _):
            lanes = pl.ds(pl.multiple_of(head * HEAD_SIZE, HEAD_SIZE), HEAD_SIZE)
            scores[head, :, rows] = lax.dot_general(
                q_buf[:, lanes], keys[rows, :], nt, preferred_element_type=F32
            )
            d_probs[head, :, rows] = lax.dot_general(
                dc_buf[:, lanes], values[rows, :], nt, preferred_element_type=F32
            )
            return 0

        lax.fori_loop(0, HEADS, one, 0, unroll=True)

    heard(1)
    greet(2)
    score(0)
    for copy in halo[:2]:
        copy.wait_recv()
    pass_on(2, 3, z_next)
    score(2)
    for copy in halo[2:4]:
        copy.wait_recv()
    score(1)
    for copy in halo[4:]:
        copy.wait_recv()
    score(3)

    second.from_left(0)
    second.from_right(1)
    second.from_left(1)
    second.from_right(0)

    lane = lax.broadcasted_iota(jnp.int32, (1, REACH * PATCHES), 1)
    image = z - lax.div(lane, PATCHES)
    is_live = (image >= span_first[0, 0]) & (image <= span_last[0, 0])
    bias = jnp.where(is_live, 0.0, -jnp.inf).astype(F32)

    def attend(head, _):
        lanes = pl.ds(pl.multiple_of(head * HEAD_SIZE, HEAD_SIZE), HEAD_SIZE)
        rows = pl.ds(pl.multiple_of(head * TOKENS, TOKENS), TOKENS)
        logits = scores[head] * SCALE + bias
        exponent = jnp.exp(logits - jnp.max(logits, axis=1, keepdims=True))
        prob = exponent * (1.0 / jnp.sum(exponent, axis=1, keepdims=True))
        prob_low = prob.astype(BF16)
        context = jnp.dot(prob_low, values[...], preferred_element_type=F32)
        att_buf[:, lanes] = (gate_tanh * context).astype(BF16)
        delta = jnp.sum(dc_buf[:, lanes].astype(F32) * context, axis=1, keepdims=True)
        d_score = (prob * (d_probs[head] - delta) * SCALE).astype(BF16)
        dq_buf[:, lanes] = jnp.dot(d_score, keys[...], preferred_element_type=F32).astype(BF16)
        p_buf[rows, :] = prob_low
        ds_buf[rows, :] = d_score
        return 0

    heard(2)
    greet(3)
    lax.fori_loop(0, HEADS, attend, 0, unroll=True)
    out_att = pltpu.make_async_copy(att_buf, attended_out.at[0], local_sems.at[4])
    out_dq = pltpu.make_async_copy(dq_buf, query_grad_out.at[0], local_sems.at[5])
    out_att.start()
    out_dq.start()

    def partial_gradients(pair):
        window = pl.ds(pair * 2 * PATCHES, 2 * PATCHES)
        for side, (left_ref, right_ref) in enumerate(((q_t, ds_buf), (dc_t, p_buf))):
            both = jnp.dot(left_ref[...], right_ref[:, window], preferred_element_type=F32)
            for index in range(2):
                tile = both[:, index * PATCHES : (index + 1) * PATCHES]
                part[pair * 2 + index, side] = jnp.transpose(tile)

    chain = []

    def hand_back(step, to):
        for side in range(2):
            copy = remote(
                chain_out.at[step, side],
                chain_in.at[step, side],
                chain_send.at[step * 2 + side],
                chain_recv.at[step * 2 + side],
                seq=to,
            )
            copy.start()
            chain.append(copy)

    partial_gradients(1)
    chain_out[0] = part[3].astype(BF16)
    hand_back(0, z_prev)
    partial_gradients(0)
    chain_out[2] = part[1].astype(BF16)
    hand_back(2, z_prev)
    second.from_opposite(0)
    second.from_opposite(1)
    for copy in chain[:2]:
        copy.wait_recv()
    chain_out[1] = (part[2] + chain_in[0].astype(F32)).astype(BF16)
    hand_back(1, z_before)
    for copy in chain[2:]:
        copy.wait_recv()
    total = part[0] + chain_in[2].astype(F32) + chain_in[1].astype(F32)
    dkv[pl.ds(0, PATCHES), pl.ds(0, HEAD_SIZE)] = total[0].astype(BF16)
    dkv[pl.ds(0, PATCHES), pl.ds(HEAD_SIZE, HEAD_SIZE)] = total[1].astype(BF16)

    shared = []
    for steps in (2, 1, 3):
        copy = remote(
            dkv.at[pl.ds(0, PATCHES), :],
            dkv.at[pl.ds(steps * PATCHES, PATCHES), :],
            dkv_send.at[steps - 1],
            dkv_recv.at[steps - 1],
            dp=lax.rem(dp + steps, DP),
        )
        copy.start()
        shared.append(copy)
    for half in (0, 1):
        second.sibling_own(half)
        for which in range(3):
            second.sibling_other(which, half)
    for copy in shared:
        copy.wait_recv()

    heard(3)

    zs = nz // TP

    def make_term(turn):
        owner = lax.rem(lax.div(z, zs) + turn, TP)
        rows = columns[owner].reshape(zs * 64, DP * PATCHES)
        result = jnp.dot(rows, dkv[...], preferred_element_type=F32)
        term[pl.ds(owner * zs, zs)] = result.reshape(zs, 64, KVC)

    lanes = ring_lanes(nz)
    height = 64 // PARTS

    def target(lane, step):
        way, base, size, _ = lane
        away = base + size - step
        return lax.rem((z + away, z + nz - away)[way], nz)

    def ring_copy(lane, step, piece):
        way, _, size, first = lane
        rows = pl.ds(piece * height, height)
        to = target(lane, step) if step == size - 1 else (z_next, z_prev)[way]
        place = first + step
        return remote(
            ring_out.at[place, rows, :],
            ring_in.at[place, rows, :],
            ring_send.at[place * PARTS + piece],
            ring_recv.at[place * PARTS + piece],
            seq=to,
        )

    def ring_step(lane, step):
        place = lane[3] + step
        for piece in range(PARTS):
            rows = pl.ds(piece * height, height)
            total = term[target(lane, step), rows, :]
            if step:
                ring_copy(lane, step - 1, piece).wait_recv()
                total += ring_in[place - 1, rows, :].astype(F32)
            ring_out[place, rows, :] = total.astype(BF16)
            ring_copy(lane, step, piece).start()

    for turn in (4, 5):
        make_term(turn)
    for lane in lanes[:2]:
        ring_step(lane, 0)
    for turn in (3, 2, 6):
        make_term(turn)
    for lane in lanes[2:4]:
        ring_step(lane, 0)
    for turn in (1, 7, 0):
        make_term(turn)
    for lane in lanes[4:]:
        ring_step(lane, 0)
    for step in range(1, max(lane[2] for lane in lanes)):
        for lane in lanes:
            if step < lane[2]:
                ring_step(lane, step)

    total = term[z]
    for lane in lanes[::-1]:
        for piece in range(PARTS):
            ring_copy(lane, lane[2] - 1, piece).wait_recv()
        total += ring_in[lane[3] + lane[2] - 1].astype(F32)
    quarter[dp] = total.astype(BF16)
    last = []
    for steps in (2, 1, 3):
        copy = remote(
            quarter.at[dp],
            quarter.at[dp],
            last_send.at[steps - 1],
            last_recv.at[steps - 1],
            dp=lax.rem(dp + steps, DP),
        )
        copy.start()
        last.append(copy)

    gather.finish()
    second.finish()
    for copy in cross + halo + chain + shared:
        copy.wait_send()

    for lane in lanes:
        for step in range(lane[2]):
            for piece in range(PARTS):
                ring_copy(lane, step, piece).wait_send()
    out_att.wait()
    out_dq.wait()
    for steps in range(1, DP):
        source = lax.rem(dp + DP - steps, DP)
        remote(
            quarter.at[source],
            quarter.at[source],
            last_send.at[steps - 1],
            last_recv.at[steps - 1],
            dp=source,
        ).wait_recv()
    for copy in last:
        copy.wait_send()
    weight_out[...] = quarter[...].reshape(DP * 64, KVC).astype(F32)


def local(nz, queries, images, kv_weight, gate, cotangent, span_first, span_last):
    zs = nz // TP
    any_space = pl.BlockSpec(memory_space=pltpu.HBM)
    vmem = pl.BlockSpec(memory_space=pltpu.VMEM)
    smem = pl.BlockSpec(memory_space=pltpu.SMEM)
    dma = pltpu.SemaphoreType.DMA
    rows = REACH * PATCHES
    low = lambda *shape: pltpu.VMEM(shape, BF16)
    hbm = lambda array: pltpu.with_memory_space_constraint(array, pltpu.HBM)
    wide = lambda *shape: pltpu.VMEM(shape, F32)
    return pl.pallas_call(
        functools.partial(kernel, nz),
        out_shape=(
            jax.ShapeDtypeStruct(queries.shape, BF16),
            jax.ShapeDtypeStruct(queries.shape, BF16),
            jax.ShapeDtypeStruct((DP * 64, KVC), F32),
        ),
        in_specs=[any_space, any_space, any_space, smem, any_space, smem, smem],
        out_specs=(any_space, any_space, vmem),
        scratch_shapes=[
            low(TOKENS, SHARD),
            low(TOKENS, SHARD),
            low(TP * SHARD, KVC),
            low(TP, PATCHES, SHARD),
            wide(PATCHES, KVC),
            low(zs, DP, 64, PATCHES),
            low(TP, zs, 64, DP * PATCHES),
            low(HEAD_SIZE, SHARD),
            low(TOKENS, SHARD),
            low(HEAD_SIZE, SHARD),
            low(rows, HEAD_SIZE),
            low(rows, HEAD_SIZE),
            wide(HEADS, TOKENS, rows),
            wide(HEADS, TOKENS, rows),
            low(HEADS * TOKENS, rows),
            low(HEADS * TOKENS, rows),
            low(TOKENS, SHARD),
            low(TOKENS, SHARD),
            wide(REACH, 2, PATCHES, HEAD_SIZE),
            low(REACH - 1, 2, PATCHES, HEAD_SIZE),
            low(REACH - 1, 2, PATCHES, HEAD_SIZE),
            low(DP * PATCHES, KVC),
            wide(nz, 64, KVC),
            low(nz - 1, 64, KVC),
            low(nz - 1, 64, KVC),
            low(DP, 64, KVC),
            dma((7,)),
            dma((GATHER_COPIES,)),
            dma((GATHER_COPIES,)),
            dma((GATHER_COPIES,)),
            dma((GATHER_COPIES,)),
            dma((DP - 1,)),
            dma((DP - 1,)),
            dma((2 * (REACH - 1),)),
            dma((2 * (REACH - 1),)),
            dma((2 * (REACH - 1),)),
            dma((2 * (REACH - 1),)),
            dma((DP - 1,)),
            dma((DP - 1,)),
            dma(((nz - 1) * PARTS,)),
            dma(((nz - 1) * PARTS,)),
            dma((DP - 1,)),
            dma((DP - 1,)),
            pltpu.SemaphoreType.REGULAR((2 * len(GREETINGS),)),
        ],
        compiler_params=pltpu.CompilerParams(
            collective_id=0, has_side_effects=True, vmem_limit_bytes=48 * 1024 * 1024
        ),
        name="cross_attention",
    )(hbm(queries), hbm(images), hbm(kv_weight), gate, hbm(cotangent), span_first, span_last)


def solution(mesh):
    return jax.shard_map(
        functools.partial(local, mesh.shape["seq"]),
        mesh=mesh,
        in_specs=(
            P("dp", "seq", "tp"),
            P("dp", "seq", None, "tp"),
            P(None, "tp"),
            P(),
            P("dp", "seq", "tp"),
            P("dp", "seq"),
            P("dp", "seq"),
        ),
        out_specs=(P("dp", "seq", "tp"), P("dp", "seq", "tp"), P("seq", "tp")),
        check_vma=False,
    )
```

```python
import functools

import jax
import jax.numpy as jnp
from jax import lax
from jax.experimental import pallas as pl
from jax.experimental.pallas import tpu as pltpu
from jax.sharding import PartitionSpec as P

HEADS = 8
HEAD_SIZE = 128
TOKENS = 128
PATCHES = 128
REACH = 4
TP = 8
DP = 4
SHARD = 1024
HALF = SHARD // 2
KVC = 2 * HEAD_SIZE
SCALE = HEAD_SIZE ** (-0.5)
GATHER_COPIES = 14
GREETINGS = (1, 2, 4, 4)
PAIR = 2
STRETCHES = ((5, 3), (4, 3))
PARTS = 2

BF16 = jnp.bfloat16
F32 = jnp.float32


def remote(src, dst, send_sem, recv_sem, **where):
    return pltpu.make_async_remote_copy(
        src_ref=src,
        dst_ref=dst,
        send_sem=send_sem,
        recv_sem=recv_sem,
        device_id=where,
        device_id_type=pl.DeviceIdType.MESH,
    )


def ring_lanes(nz):
    lanes, slot = [], 0
    for way in range(2):
        base = 0
        for size in STRETCHES[way]:
            lanes.append((way, base, size, slot))
            base, slot = base + size, slot + size
        assert base == nz // (2 * PAIR) - way
    return sorted(lanes, key=lambda lane: -lane[1] - lane[2])


class RowGather:
    def __init__(self, own, slot, send_sems, recv_sems):
        tp = lax.axis_index("tp")
        self.tp = tp
        self.right, self.left = lax.rem(tp + 2, TP), lax.rem(tp + TP - 2, TP)
        self.opposite = lax.rem(tp + 4, TP)
        self.sibling = tp + 1 - 2 * lax.rem(tp, 2)
        self.own, self.slot = own, slot
        self.send_sems, self.recv_sems = send_sems, recv_sems
        self.started = []

    def _copy(self, index, src, dst, target):
        return remote(src, dst, self.send_sems.at[index], self.recv_sems.at[index], tp=target)

    def _start(self, index, src, owner, half, target):
        copy = self._copy(index, src, self.slot(owner, half), target)
        copy.start()
        self.started.append(copy)

    def _arrived(self, index, owner, half):
        ref = self.slot(owner, half)
        self._copy(index, ref, ref, self.right).wait_recv()

    def send_own(self):
        for half in (0, 1):
            self._start(half, self.own(half), self.tp, half, self.right)
            self._start(3 - half, self.own(1 - half), self.tp, 1 - half, self.left)
        for half in (0, 1):
            self._start(6 + half, self.own(half), self.tp, half, self.sibling)

    def sibling_own(self, half):
        self._arrived(6 + half, self.sibling, half)
        return self.sibling, half

    def from_left(self, half):
        self._arrived(half, self.left, half)
        ref = self.slot(self.left, half)
        if half == 0:
            self._start(4, ref, self.left, half, self.right)
        self._start(8 + half, ref, self.left, half, self.sibling)
        return self.left, half

    def from_right(self, half):
        self._arrived(2 + half, self.right, half)
        ref = self.slot(self.right, half)
        if half == 1:
            self._start(5, ref, self.right, half, self.left)
        self._start(10 + half, ref, self.right, half, self.sibling)
        return self.right, half

    def from_opposite(self, half):
        self._arrived(4 + half, self.opposite, half)
        self._start(12 + half, self.slot(self.opposite, half), self.opposite, half, self.sibling)
        return self.opposite, half

    def sibling_other(self, which, half):
        owner = lax.rem(self.sibling + (TP - 2, 2, 4)[which], TP)
        self._arrived(8 + 2 * which + half, owner, half)
        return owner, half

    def finish(self):
        for copy in self.started:
            copy.wait_send()


def kernel(
    nz,
    queries,
    features,
    kv_weight,
    gate,
    cotangent,
    span_first,
    span_last,
    attended_out,
    query_grad_out,
    weight_out,
    q_buf,
    cot_buf,
    w_buf,
    gathered,
    proj,
    transposed,
    columns,
    q_t,
    dc_buf,
    dc_t,
    keys,
    values,
    scores,
    d_probs,
    p_buf,
    ds_buf,
    att_buf,
    dq_buf,
    part,
    chain_out,
    chain_in,
    dkv,
    term,
    ring_out,
    ring_in,
    quarter,
    local_sems,
    feat_send,
    feat_recv,
    col_send,
    col_recv,
    cross_send,
    cross_recv,
    kv_send,
    kv_recv,
    chain_send,
    chain_recv,
    dkv_send,
    dkv_recv,
    ring_send,
    ring_recv,
    last_send,
    last_recv,
    greeted,
):
    z, tp, dp = lax.axis_index("seq"), lax.axis_index("tp"), lax.axis_index("dp")
    z_next, z_prev = lax.rem(z + 1, nz), lax.rem(z + nz - 1, nz)
    z_after, z_before = lax.rem(z + 2, nz), lax.rem(z + nz - 2, nz)
    parity = lax.rem(z, PAIR)
    partner = z + 1 - 2 * parity
    peers = [(side, steps) for side, steps in ((1, 2), (0, 2), (1, 1), (1, 3), (0, 1), (0, 3), (1, 0))]

    def peer(side, steps):
        return {"seq": (z, partner)[side], "dp": lax.rem(dp + steps, DP)}

    in_q = pltpu.make_async_copy(queries.at[0], q_buf, local_sems.at[0])
    in_cot = pltpu.make_async_copy(cotangent.at[0], cot_buf, local_sems.at[1])
    in_w = pltpu.make_async_copy(kv_weight, w_buf, local_sems.at[2])
    in_f = pltpu.make_async_copy(features.at[0, 0], gathered.at[lax.axis_index('tp')], local_sems.at[6])
    in_f.start()
    in_q.start()
    in_cot.start()
    in_w.start()

    gather = RowGather(
        lambda half: features.at[0, 0, :, pl.ds(half * HALF, HALF)],
        lambda owner, half: gathered.at[owner, :, pl.ds(half * HALF, HALF)],
        feat_send,
        feat_recv,
    )
    barrier = pltpu.get_barrier_semaphore()
    mesh_id = pl.DeviceIdType.MESH
    for other in (gather.right, gather.left, gather.sibling):
        pl.semaphore_signal(barrier, inc=1, device_id={"tp": other}, device_id_type=mesh_id)
    for steps in range(1, DP):
        other = lax.rem(dp + steps, DP)
        pl.semaphore_signal(barrier, inc=1, device_id={"dp": other}, device_id_type=mesh_id)
        pl.semaphore_signal(barrier, inc=1, device_id=peer(1, steps), device_id_type=mesh_id)
    for other in (z_next, z_prev):
        pl.semaphore_signal(barrier, inc=1, device_id={"seq": other}, device_id_type=mesh_id)
    pl.semaphore_wait(barrier, 11)

    def greet(turn):
        for way in range(2):
            step = GREETINGS[turn]
            other = lax.rem((z + step, z + nz - step)[way], nz)
            pl.semaphore_signal(greeted.at[turn * 2 + way], inc=1, device_id={"seq": other}, device_id_type=mesh_id)

    def heard(turn):
        for way in range(2):
            pl.semaphore_wait(greeted.at[turn * 2 + way], 1)

    gather.send_own()
    greet(0)
    in_f.wait()

    for block in range(SHARD // 128):
        tile = gathered[tp, :, block * 128 : (block + 1) * 128].astype(F32)
        flipped = jnp.transpose(tile).astype(BF16)
        for piece in range(2):
            place = block * 2 + piece
            row = place // DP
            transposed[row % PAIR, row // PAIR, place % DP] = flipped[piece * 64 : (piece + 1) * 64]
    own_quarter = pltpu.make_async_copy(
        transposed.at[parity, :, dp], columns.at[tp, :, :, pl.ds(0, 128)], local_sems.at[3]
    )
    own_quarter.start()
    cross = []
    for side, steps in peers:
        place = side * DP + steps
        where = peer(side, steps)
        copy = remote(
            transposed.at[(parity, 1 - parity)[side], :, where["dp"]],
            columns.at[tp, :, :, pl.ds(place * 128, 128)],
            cross_send.at[place - 1],
            cross_recv.at[place - 1],
            **where,
        )
        copy.start()
        cross.append(copy)

    in_w.wait()

    def project(owner, half):
        rows = pl.ds(pl.multiple_of(owner * SHARD + half * HALF, HALF), HALF)
        block = gathered[owner, :, half * HALF : (half + 1) * HALF]
        return jnp.dot(block, w_buf[rows, :], preferred_element_type=F32)

    proj[...] = project(tp, 0) + project(tp, 1)
    for half in (0, 1):
        proj[...] += project(*gather.sibling_own(half))

    in_q.wait()
    in_cot.wait()
    gate_tanh = jnp.tanh(jnp.full((8, 128), gate[0], F32))[:1]

    def prepare(head, _):
        lanes = pl.ds(pl.multiple_of(head * HEAD_SIZE, HEAD_SIZE), HEAD_SIZE)
        low = (gate_tanh * cot_buf[:, lanes].astype(F32)).astype(BF16)
        dc_buf[:, lanes] = low
        dc_t[:, lanes] = jnp.transpose(low.astype(F32)).astype(BF16)
        q_t[:, lanes] = jnp.transpose(q_buf[:, lanes].astype(F32)).astype(BF16)
        return 0

    lax.fori_loop(0, HEADS, prepare, 0, unroll=True)
    heard(0)
    greet(1)

    arrived = [gather.from_left(0), gather.from_right(1)]
    for owner, half in arrived:
        proj[...] += project(owner, half)
    arrived = [gather.from_left(1), gather.from_right(0)]
    for owner, half in arrived:
        proj[...] += project(owner, half)
    for which, half in ((0, 0), (1, 1), (0, 1), (1, 0)):
        proj[...] += project(*gather.sibling_other(which, half))
    arrived = [gather.from_opposite(0), gather.from_opposite(1)]
    for owner, half in arrived:
        proj[...] += project(owner, half)
    for half in (0, 1):
        proj[...] += project(*gather.sibling_other(2, half))

    keys[pl.ds(0, PATCHES), :] = proj[:, :HEAD_SIZE].astype(BF16)
    values[pl.ds(0, PATCHES), :] = proj[:, HEAD_SIZE:].astype(BF16)

    halo = []

    def pass_on(source, offset, to):
        for side, rows in enumerate((keys, values)):
            copy = remote(
                rows.at[pl.ds(source * PATCHES, PATCHES), :],
                rows.at[pl.ds(offset * PATCHES, PATCHES), :],
                kv_send.at[offset * 2 - 2 + side],
                kv_recv.at[offset * 2 - 2 + side],
                seq=to,
            )
            copy.start()
            halo.append(copy)

    pass_on(0, 2, z_after)
    pass_on(0, 1, z_next)

    own_quarter.wait()
    for copy in cross:
        copy.wait_recv()
    second = RowGather(
        lambda half: columns.at[tp, pl.ds(half, 1)],
        lambda owner, half: columns.at[owner, pl.ds(half, 1)],
        col_send,
        col_recv,
    )
    second.send_own()

    def score(offset):
        rows = pl.ds(offset * PATCHES, PATCHES)
        nt = (((1,), (1,)), ((), ()))

        def one(head, _):
            lanes = pl.ds(pl.multiple_of(head * HEAD_SIZE, HEAD_SIZE), HEAD_SIZE)
            scores[head, :, rows] = lax.dot_general(
                q_buf[:, lanes], keys[rows, :], nt, preferred_element_type=F32
            )
            d_probs[head, :, rows] = lax.dot_general(
                dc_buf[:, lanes], values[rows, :], nt, preferred_element_type=F32
            )
            return 0

        lax.fori_loop(0, HEADS, one, 0, unroll=True)

    heard(1)
    greet(2)
    score(0)
    for copy in halo[:2]:
        copy.wait_recv()
    pass_on(2, 3, z_next)
    score(2)
    for copy in halo[2:4]:
        copy.wait_recv()
    score(1)
    for copy in halo[4:]:
        copy.wait_recv()
    score(3)

    second.from_left(0)
    second.from_right(1)
    second.from_left(1)
    second.from_right(0)

    lane = lax.broadcasted_iota(jnp.int32, (1, REACH * PATCHES), 1)
    image = z - lax.div(lane, PATCHES)
    is_live = (image >= span_first[0, 0]) & (image <= span_last[0, 0])
    bias = jnp.where(is_live, 0.0, -jnp.inf).astype(F32)

    def attend(head, _):
        lanes = pl.ds(pl.multiple_of(head * HEAD_SIZE, HEAD_SIZE), HEAD_SIZE)
        rows = pl.ds(pl.multiple_of(head * TOKENS, TOKENS), TOKENS)
        logits = scores[head] * SCALE + bias
        exponent = jnp.exp(logits - jnp.max(logits, axis=1, keepdims=True))
        prob = exponent * (1.0 / jnp.sum(exponent, axis=1, keepdims=True))
        prob_low = prob.astype(BF16)
        context = jnp.dot(prob_low, values[...], preferred_element_type=F32)
        att_buf[:, lanes] = (gate_tanh * context).astype(BF16)
        delta = jnp.sum(dc_buf[:, lanes].astype(F32) * context, axis=1, keepdims=True)
        d_score = (prob * (d_probs[head] - delta) * SCALE).astype(BF16)
        dq_buf[:, lanes] = jnp.dot(d_score, keys[...], preferred_element_type=F32).astype(BF16)
        p_buf[rows, :] = prob_low
        ds_buf[rows, :] = d_score
        return 0

    heard(2)
    greet(3)
    lax.fori_loop(0, HEADS, attend, 0, unroll=True)
    out_att = pltpu.make_async_copy(att_buf, attended_out.at[0], local_sems.at[4])
    out_dq = pltpu.make_async_copy(dq_buf, query_grad_out.at[0], local_sems.at[5])
    out_att.start()
    out_dq.start()

    def partial_gradients(pair):
        window = pl.ds(pair * 2 * PATCHES, 2 * PATCHES)
        for side, (left_ref, right_ref) in enumerate(((q_t, ds_buf), (dc_t, p_buf))):
            both = jnp.dot(left_ref[...], right_ref[:, window], preferred_element_type=F32)
            for index in range(2):
                tile = both[:, index * PATCHES : (index + 1) * PATCHES]
                part[pair * 2 + index, side] = jnp.transpose(tile)

    chain = []

    def hand_back(step, to):
        for side in range(2):
            copy = remote(
                chain_out.at[step, side],
                chain_in.at[step, side],
                chain_send.at[step * 2 + side],
                chain_recv.at[step * 2 + side],
                seq=to,
            )
            copy.start()
            chain.append(copy)

    partial_gradients(1)
    chain_out[0] = part[3].astype(BF16)
    hand_back(0, z_prev)
    partial_gradients(0)
    chain_out[2] = part[1].astype(BF16)
    hand_back(2, z_prev)
    second.from_opposite(0)
    second.from_opposite(1)
    for copy in chain[:2]:
        copy.wait_recv()
    chain_out[1] = (part[2] + chain_in[0].astype(F32)).astype(BF16)
    hand_back(1, z_before)
    for copy in chain[2:]:
        copy.wait_recv()
    total = part[0] + chain_in[2].astype(F32) + chain_in[1].astype(F32)
    dkv[pl.ds(0, PATCHES), pl.ds(0, HEAD_SIZE)] = total[0].astype(BF16)
    dkv[pl.ds(0, PATCHES), pl.ds(HEAD_SIZE, HEAD_SIZE)] = total[1].astype(BF16)

    shared = []
    for side, steps in peers:
        place = side * DP + steps
        copy = remote(
            dkv.at[pl.ds(0, PATCHES), :],
            dkv.at[pl.ds(place * PATCHES, PATCHES), :],
            dkv_send.at[place - 1],
            dkv_recv.at[place - 1],
            **peer(side, steps),
        )
        copy.start()
        shared.append(copy)
    for half in (0, 1):
        second.sibling_own(half)
        for which in range(3):
            second.sibling_other(which, half)
    for copy in shared:
        copy.wait_recv()

    heard(3)

    zs = nz // TP // PAIR
    members = nz // PAIR
    member = lax.div(z, PAIR)

    def make_term(turn):
        owner = lax.rem(lax.div(member, zs) + turn, TP)
        rows = columns[owner].reshape(zs * 64, PAIR * DP * PATCHES)
        result = jnp.dot(rows, dkv[...], preferred_element_type=F32)
        term[pl.ds(owner * zs, zs)] = result.reshape(zs, 64, KVC)

    lanes = ring_lanes(nz)
    height = 64 // PARTS

    def target(lane, step):
        way, base, size, _ = lane
        away = base + size - step
        return lax.rem((member + away, member + members - away)[way], members)

    def ring_copy(lane, step, piece):
        way, _, size, first = lane
        rows = pl.ds(piece * height, height)
        to = target(lane, step) * PAIR + parity if step == size - 1 else (z_after, z_before)[way]
        place = first + step
        return remote(
            ring_out.at[place, rows, :],
            ring_in.at[place, rows, :],
            ring_send.at[place * PARTS + piece],
            ring_recv.at[place * PARTS + piece],
            seq=to,
        )

    def ring_step(lane, step):
        place = lane[3] + step
        for piece in range(PARTS):
            rows = pl.ds(piece * height, height)
            total = term[target(lane, step), rows, :]
            if step:
                ring_copy(lane, step - 1, piece).wait_recv()
                total += ring_in[place - 1, rows, :].astype(F32)
            ring_out[place, rows, :] = total.astype(BF16)
            ring_copy(lane, step, piece).start()

    for turn in (4, 5):
        make_term(turn)
    for lane in lanes[:2]:
        ring_step(lane, 0)
    for turn in (3, 2, 6):
        make_term(turn)
    for lane in lanes[2:4]:
        ring_step(lane, 0)
    for turn in (1, 7, 0):
        make_term(turn)
    for lane in lanes[4:]:
        ring_step(lane, 0)
    for step in range(1, max(lane[2] for lane in lanes)):
        for lane in lanes:
            if step < lane[2]:
                ring_step(lane, step)

    total = term[member]
    for lane in lanes[::-1]:
        for piece in range(PARTS):
            ring_copy(lane, lane[2] - 1, piece).wait_recv()
        total += ring_in[lane[3] + lane[2] - 1].astype(F32)
    quarter[dp] = total.astype(BF16)
    last = []
    for steps in (2, 1, 3):
        copy = remote(
            quarter.at[dp],
            quarter.at[dp],
            last_send.at[steps - 1],
            last_recv.at[steps - 1],
            dp=lax.rem(dp + steps, DP),
        )
        copy.start()
        last.append(copy)

    gather.finish()
    second.finish()
    for copy in cross + halo + chain + shared:
        copy.wait_send()

    for lane in lanes:
        for step in range(lane[2]):
            for piece in range(PARTS):
                ring_copy(lane, step, piece).wait_send()
    out_att.wait()
    out_dq.wait()
    for steps in range(1, DP):
        source = lax.rem(dp + DP - steps, DP)
        remote(
            quarter.at[source],
            quarter.at[source],
            last_send.at[steps - 1],
            last_recv.at[steps - 1],
            dp=source,
        ).wait_recv()
    for copy in last:
        copy.wait_send()
    weight_out[...] = quarter[...].reshape(DP * 64, KVC).astype(F32)


def local(nz, queries, images, kv_weight, gate, cotangent, span_first, span_last):
    zs = nz // TP
    any_space = pl.BlockSpec(memory_space=pltpu.HBM)
    vmem = pl.BlockSpec(memory_space=pltpu.VMEM)
    smem = pl.BlockSpec(memory_space=pltpu.SMEM)
    dma = pltpu.SemaphoreType.DMA
    rows = REACH * PATCHES
    low = lambda *shape: pltpu.VMEM(shape, BF16)
    hbm = lambda array: pltpu.with_memory_space_constraint(array, pltpu.HBM)
    wide = lambda *shape: pltpu.VMEM(shape, F32)
    return pl.pallas_call(
        functools.partial(kernel, nz),
        out_shape=(
            jax.ShapeDtypeStruct(queries.shape, BF16),
            jax.ShapeDtypeStruct(queries.shape, BF16),
            jax.ShapeDtypeStruct((DP * 64, KVC), F32),
        ),
        in_specs=[any_space, any_space, any_space, smem, any_space, smem, smem],
        out_specs=(any_space, any_space, vmem),
        scratch_shapes=[
            low(TOKENS, SHARD),
            low(TOKENS, SHARD),
            low(TP * SHARD, KVC),
            low(TP, PATCHES, SHARD),
            wide(PATCHES, KVC),
            low(PAIR, zs // PAIR, DP, 64, PATCHES),
            low(TP, zs // PAIR, 64, PAIR * DP * PATCHES),
            low(HEAD_SIZE, SHARD),
            low(TOKENS, SHARD),
            low(HEAD_SIZE, SHARD),
            low(rows, HEAD_SIZE),
            low(rows, HEAD_SIZE),
            wide(HEADS, TOKENS, rows),
            wide(HEADS, TOKENS, rows),
            low(HEADS * TOKENS, rows),
            low(HEADS * TOKENS, rows),
            low(TOKENS, SHARD),
            low(TOKENS, SHARD),
            wide(REACH, 2, PATCHES, HEAD_SIZE),
            low(REACH - 1, 2, PATCHES, HEAD_SIZE),
            low(REACH - 1, 2, PATCHES, HEAD_SIZE),
            low(PAIR * DP * PATCHES, KVC),
            wide(nz // PAIR, 64, KVC),
            low(nz // PAIR - 1, 64, KVC),
            low(nz // PAIR - 1, 64, KVC),
            low(DP, 64, KVC),
            dma((7,)),
            dma((GATHER_COPIES,)),
            dma((GATHER_COPIES,)),
            dma((GATHER_COPIES,)),
            dma((GATHER_COPIES,)),
            dma((PAIR * DP - 1,)),
            dma((PAIR * DP - 1,)),
            dma((2 * (REACH - 1),)),
            dma((2 * (REACH - 1),)),
            dma((2 * (REACH - 1),)),
            dma((2 * (REACH - 1),)),
            dma((PAIR * DP - 1,)),
            dma((PAIR * DP - 1,)),
            dma(((nz // PAIR - 1) * PARTS,)),
            dma(((nz // PAIR - 1) * PARTS,)),
            dma((DP - 1,)),
            dma((DP - 1,)),
            pltpu.SemaphoreType.REGULAR((2 * len(GREETINGS),)),
        ],
        compiler_params=pltpu.CompilerParams(
            collective_id=0, has_side_effects=True, vmem_limit_bytes=48 * 1024 * 1024
        ),
        name="cross_attention",
    )(hbm(queries), hbm(images), hbm(kv_weight), gate, hbm(cotangent), span_first, span_last)


def solution(mesh):
    return jax.shard_map(
        functools.partial(local, mesh.shape["seq"]),
        mesh=mesh,
        in_specs=(
            P("dp", "seq", "tp"),
            P("dp", "seq", None, "tp"),
            P(None, "tp"),
            P(),
            P("dp", "seq", "tp"),
            P("dp", "seq"),
            P("dp", "seq"),
        ),
        out_specs=(P("dp", "seq", "tp"), P("dp", "seq", "tp"), P("seq", "tp")),
        check_vma=False,
    )
```

```python
import functools

import jax
import jax.numpy as jnp
from jax import lax
from jax.experimental import pallas as pl
from jax.experimental.pallas import tpu as pltpu
from jax.sharding import PartitionSpec as P

HEADS = 8
HEAD_SIZE = 128
TOKENS = 128
PATCHES = 128
REACH = 4
TP = 8
DP = 4
SHARD = 1024
HALF = SHARD // 2
KVC = 2 * HEAD_SIZE
SCALE = HEAD_SIZE ** (-0.5)
GATHER_COPIES = 14
GREETINGS = (1, 2, 4, 4)
PAIR = 2
STRETCHES = ((5, 3), (4, 3))
PARTS = 2

BF16 = jnp.bfloat16
F32 = jnp.float32


def remote(src, dst, send_sem, recv_sem, **where):
    return pltpu.make_async_remote_copy(
        src_ref=src,
        dst_ref=dst,
        send_sem=send_sem,
        recv_sem=recv_sem,
        device_id=where,
        device_id_type=pl.DeviceIdType.MESH,
    )


def ring_lanes(nz):
    lanes, slot = [], 0
    for way in range(2):
        base = 0
        for size in STRETCHES[way]:
            lanes.append((way, base, size, slot))
            base, slot = base + size, slot + size
        assert base == nz // (2 * PAIR) - way
    return sorted(lanes, key=lambda lane: -lane[1] - lane[2])


class RowGather:
    def __init__(self, own, slot, send_sems, recv_sems):
        tp = lax.axis_index("tp")
        self.tp = tp
        self.right, self.left = lax.rem(tp + 2, TP), lax.rem(tp + TP - 2, TP)
        self.opposite = lax.rem(tp + 4, TP)
        self.sibling = tp + 1 - 2 * lax.rem(tp, 2)
        self.own, self.slot = own, slot
        self.send_sems, self.recv_sems = send_sems, recv_sems
        self.started = []

    def _copy(self, index, src, dst, target):
        return remote(src, dst, self.send_sems.at[index], self.recv_sems.at[index], tp=target)

    def _start(self, index, src, owner, half, target):
        copy = self._copy(index, src, self.slot(owner, half), target)
        copy.start()
        self.started.append(copy)

    def _arrived(self, index, owner, half):
        ref = self.slot(owner, half)
        self._copy(index, ref, ref, self.right).wait_recv()

    def send_own(self):
        for half in (0, 1):
            self._start(half, self.own(half), self.tp, half, self.right)
            self._start(3 - half, self.own(1 - half), self.tp, 1 - half, self.left)
        for half in (0, 1):
            self._start(6 + half, self.own(half), self.tp, half, self.sibling)

    def sibling_own(self, half):
        self._arrived(6 + half, self.sibling, half)
        return self.sibling, half

    def from_left(self, half):
        self._arrived(half, self.left, half)
        ref = self.slot(self.left, half)
        if half == 0:
            self._start(4, ref, self.left, half, self.right)
        self._start(8 + half, ref, self.left, half, self.sibling)
        return self.left, half

    def from_right(self, half):
        self._arrived(2 + half, self.right, half)
        ref = self.slot(self.right, half)
        if half == 1:
            self._start(5, ref, self.right, half, self.left)
        self._start(10 + half, ref, self.right, half, self.sibling)
        return self.right, half

    def from_opposite(self, half):
        self._arrived(4 + half, self.opposite, half)
        self._start(12 + half, self.slot(self.opposite, half), self.opposite, half, self.sibling)
        return self.opposite, half

    def sibling_other(self, which, half):
        owner = lax.rem(self.sibling + (TP - 2, 2, 4)[which], TP)
        self._arrived(8 + 2 * which + half, owner, half)
        return owner, half

    def finish(self):
        for copy in self.started:
            copy.wait_send()


def kernel(
    nz,
    queries,
    features,
    kv_weight,
    gate,
    cotangent,
    span_first,
    span_last,
    attended_out,
    query_grad_out,
    weight_out,
    q_buf,
    cot_buf,
    w_buf,
    gathered,
    proj,
    transposed,
    columns,
    q_t,
    dc_buf,
    dc_t,
    keys,
    values,
    scores,
    d_probs,
    p_buf,
    ds_buf,
    att_buf,
    dq_buf,
    part,
    chain_out,
    chain_in,
    dkv,
    term,
    ring_out,
    ring_in,
    quarter,
    local_sems,
    feat_send,
    feat_recv,
    col_send,
    col_recv,
    cross_send,
    cross_recv,
    kv_send,
    kv_recv,
    chain_send,
    chain_recv,
    dkv_send,
    dkv_recv,
    ring_send,
    ring_recv,
    last_send,
    last_recv,
    greeted,
):
    z, tp, dp = lax.axis_index("seq"), lax.axis_index("tp"), lax.axis_index("dp")
    z_next, z_prev = lax.rem(z + 1, nz), lax.rem(z + nz - 1, nz)
    z_after, z_before = lax.rem(z + 2, nz), lax.rem(z + nz - 2, nz)
    parity = lax.rem(z, PAIR)
    partner = z + 1 - 2 * parity
    peers = [(side, steps) for side, steps in ((1, 2), (0, 2), (1, 1), (1, 3), (0, 1), (0, 3), (1, 0))]

    def peer(side, steps):
        return {"seq": (z, partner)[side], "dp": lax.rem(dp + steps, DP)}

    in_q = pltpu.make_async_copy(queries.at[0], q_buf, local_sems.at[0])
    in_cot = pltpu.make_async_copy(cotangent.at[0], cot_buf, local_sems.at[1])
    in_w = pltpu.make_async_copy(kv_weight, w_buf, local_sems.at[2])
    in_f = pltpu.make_async_copy(features.at[0, 0], gathered.at[lax.axis_index('tp')], local_sems.at[6])
    in_f.start()
    in_q.start()
    in_cot.start()
    in_w.start()

    gather = RowGather(
        lambda half: features.at[0, 0, :, pl.ds(half * HALF, HALF)],
        lambda owner, half: gathered.at[owner, :, pl.ds(half * HALF, HALF)],
        feat_send,
        feat_recv,
    )
    barrier = pltpu.get_barrier_semaphore()
    mesh_id = pl.DeviceIdType.MESH
    for other in (gather.right, gather.left, gather.sibling):
        pl.semaphore_signal(barrier, inc=1, device_id={"tp": other}, device_id_type=mesh_id)
    for steps in range(1, DP):
        other = lax.rem(dp + steps, DP)
        pl.semaphore_signal(barrier, inc=1, device_id={"dp": other}, device_id_type=mesh_id)
        pl.semaphore_signal(barrier, inc=1, device_id=peer(1, steps), device_id_type=mesh_id)
    for other in (z_next, z_prev):
        pl.semaphore_signal(barrier, inc=1, device_id={"seq": other}, device_id_type=mesh_id)
    pl.semaphore_wait(barrier, 11)

    def greet(turn):
        for way in range(2):
            step = GREETINGS[turn]
            other = lax.rem((z + step, z + nz - step)[way], nz)
            pl.semaphore_signal(greeted.at[turn * 2 + way], inc=1, device_id={"seq": other}, device_id_type=mesh_id)

    def heard(turn):
        for way in range(2):
            pl.semaphore_wait(greeted.at[turn * 2 + way], 1)

    gather.send_own()
    greet(0)
    in_f.wait()

    for block in range(SHARD // 128):
        tile = gathered[tp, :, block * 128 : (block + 1) * 128].astype(F32)
        flipped = jnp.transpose(tile).astype(BF16)
        for piece in range(2):
            place = block * 2 + piece
            row = place // DP
            transposed[row % PAIR, row // PAIR, place % DP] = flipped[piece * 64 : (piece + 1) * 64]
    own_quarter = pltpu.make_async_copy(
        transposed.at[parity, :, dp], columns.at[tp, :, :, pl.ds(0, 128)], local_sems.at[3]
    )
    own_quarter.start()
    cross = []
    for side, steps in peers:
        place = side * DP + steps
        where = peer(side, steps)
        copy = remote(
            transposed.at[(parity, 1 - parity)[side], :, where["dp"]],
            columns.at[tp, :, :, pl.ds(place * 128, 128)],
            cross_send.at[place - 1],
            cross_recv.at[place - 1],
            **where,
        )
        copy.start()
        cross.append(copy)

    in_w.wait()

    def project(owner, half):
        rows = pl.ds(pl.multiple_of(owner * SHARD + half * HALF, HALF), HALF)
        block = gathered[owner, :, half * HALF : (half + 1) * HALF]
        return jnp.dot(block, w_buf[rows, :], preferred_element_type=F32)

    proj[...] = project(tp, 0) + project(tp, 1)
    for half in (0, 1):
        proj[...] += project(*gather.sibling_own(half))

    in_q.wait()
    in_cot.wait()
    gate_tanh = jnp.tanh(jnp.full((8, 128), gate[0], F32))[:1]

    def prepare(head, _):
        lanes = pl.ds(pl.multiple_of(head * HEAD_SIZE, HEAD_SIZE), HEAD_SIZE)
        low = (gate_tanh * cot_buf[:, lanes].astype(F32)).astype(BF16)
        dc_buf[:, lanes] = low
        dc_t[:, lanes] = jnp.transpose(low.astype(F32)).astype(BF16)
        q_t[:, lanes] = jnp.transpose(q_buf[:, lanes].astype(F32)).astype(BF16)
        return 0

    lax.fori_loop(0, HEADS, prepare, 0, unroll=True)
    heard(0)
    greet(1)

    arrived = [gather.from_left(0), gather.from_right(1)]
    for owner, half in arrived:
        proj[...] += project(owner, half)
    arrived = [gather.from_left(1), gather.from_right(0)]
    for owner, half in arrived:
        proj[...] += project(owner, half)
    for which, half in ((0, 0), (1, 1), (0, 1), (1, 0)):
        proj[...] += project(*gather.sibling_other(which, half))
    arrived = [gather.from_opposite(0), gather.from_opposite(1)]
    for owner, half in arrived:
        proj[...] += project(owner, half)
    for half in (0, 1):
        proj[...] += project(*gather.sibling_other(2, half))

    keys[pl.ds(0, PATCHES), :] = proj[:, :HEAD_SIZE].astype(BF16)
    values[pl.ds(0, PATCHES), :] = proj[:, HEAD_SIZE:].astype(BF16)

    halo = []

    def pass_on(source, offset, to, sides=(0, 1)):
        for side in sides:
            rows = (keys, values)[side]
            copy = remote(
                rows.at[pl.ds(source * PATCHES, PATCHES), :],
                rows.at[pl.ds(offset * PATCHES, PATCHES), :],
                kv_send.at[offset * 2 - 2 + side],
                kv_recv.at[offset * 2 - 2 + side],
                seq=to,
            )
            copy.start()
            halo.append(copy)

    pass_on(0, 2, z_after)
    pass_on(0, 1, z_next)

    own_quarter.wait()
    for copy in cross:
        copy.wait_recv()
    second = RowGather(
        lambda half: columns.at[tp, pl.ds(half, 1)],
        lambda owner, half: columns.at[owner, pl.ds(half, 1)],
        col_send,
        col_recv,
    )
    second.send_own()

    def score(offset):
        rows = pl.ds(offset * PATCHES, PATCHES)
        nt = (((1,), (1,)), ((), ()))

        def one(head, _):
            lanes = pl.ds(pl.multiple_of(head * HEAD_SIZE, HEAD_SIZE), HEAD_SIZE)
            scores[head, :, rows] = lax.dot_general(
                q_buf[:, lanes], keys[rows, :], nt, preferred_element_type=F32
            )
            d_probs[head, :, rows] = lax.dot_general(
                dc_buf[:, lanes], values[rows, :], nt, preferred_element_type=F32
            )
            return 0

        lax.fori_loop(0, HEADS, one, 0, unroll=True)

    heard(1)
    greet(2)
    score(0)
    for side in range(2):
        halo[side].wait_recv()
        pass_on(2, 3, z_next, (side,))
    score(2)
    for copy in halo[2:4]:
        copy.wait_recv()
    score(1)
    for copy in halo[4:]:
        copy.wait_recv()
    score(3)

    second.from_left(0)
    second.from_right(1)
    second.from_left(1)
    second.from_right(0)

    lane = lax.broadcasted_iota(jnp.int32, (1, REACH * PATCHES), 1)
    image = z - lax.div(lane, PATCHES)
    is_live = (image >= span_first[0, 0]) & (image <= span_last[0, 0])
    bias = jnp.where(is_live, 0.0, -jnp.inf).astype(F32)

    def attend(head, _):
        lanes = pl.ds(pl.multiple_of(head * HEAD_SIZE, HEAD_SIZE), HEAD_SIZE)
        rows = pl.ds(pl.multiple_of(head * TOKENS, TOKENS), TOKENS)
        logits = scores[head] * SCALE + bias
        exponent = jnp.exp(logits - jnp.max(logits, axis=1, keepdims=True))
        prob = exponent * (1.0 / jnp.sum(exponent, axis=1, keepdims=True))
        prob_low = prob.astype(BF16)
        context = jnp.dot(prob_low, values[...], preferred_element_type=F32)
        att_buf[:, lanes] = (gate_tanh * context).astype(BF16)
        delta = jnp.sum(dc_buf[:, lanes].astype(F32) * context, axis=1, keepdims=True)
        d_score = (prob * (d_probs[head] - delta) * SCALE).astype(BF16)
        dq_buf[:, lanes] = jnp.dot(d_score, keys[...], preferred_element_type=F32).astype(BF16)
        p_buf[rows, :] = prob_low
        ds_buf[rows, :] = d_score
        return 0

    heard(2)
    greet(3)
    lax.fori_loop(0, HEADS, attend, 0, unroll=True)
    out_att = pltpu.make_async_copy(att_buf, attended_out.at[0], local_sems.at[4])
    out_dq = pltpu.make_async_copy(dq_buf, query_grad_out.at[0], local_sems.at[5])
    out_att.start()
    out_dq.start()

    def partial_gradients(pair, sides=(0, 1)):
        window = pl.ds(pair * 2 * PATCHES, 2 * PATCHES)
        for side in sides:
            left_ref, right_ref = ((q_t, ds_buf), (dc_t, p_buf))[side]
            both = jnp.dot(left_ref[...], right_ref[:, window], preferred_element_type=F32)
            for index in range(2):
                tile = both[:, index * PATCHES : (index + 1) * PATCHES]
                part[pair * 2 + index, side] = jnp.transpose(tile)

    chain = []

    def hand_back(step, to, sides=(0, 1)):
        for side in sides:
            copy = remote(
                chain_out.at[step, side],
                chain_in.at[step, side],
                chain_send.at[step * 2 + side],
                chain_recv.at[step * 2 + side],
                seq=to,
            )
            copy.start()
            chain.append(copy)

    for side in range(2):
        partial_gradients(1, (side,))
        chain_out[0, side] = part[3, side].astype(BF16)
        hand_back(0, z_prev, (side,))
    partial_gradients(0)
    chain_out[2] = part[1].astype(BF16)
    hand_back(2, z_prev)
    second.from_opposite(0)
    second.from_opposite(1)
    for side in range(2):
        chain[side].wait_recv()
        chain_out[1, side] = (part[2, side] + chain_in[0, side].astype(F32)).astype(BF16)
        hand_back(1, z_before, (side,))
    for copy in chain[2:]:
        copy.wait_recv()
    total = part[0] + chain_in[2].astype(F32) + chain_in[1].astype(F32)
    dkv[pl.ds(0, PATCHES), pl.ds(0, HEAD_SIZE)] = total[0].astype(BF16)
    dkv[pl.ds(0, PATCHES), pl.ds(HEAD_SIZE, HEAD_SIZE)] = total[1].astype(BF16)

    shared = []
    for side, steps in peers:
        place = side * DP + steps
        copy = remote(
            dkv.at[pl.ds(0, PATCHES), :],
            dkv.at[pl.ds(place * PATCHES, PATCHES), :],
            dkv_send.at[place - 1],
            dkv_recv.at[place - 1],
            **peer(side, steps),
        )
        copy.start()
        shared.append(copy)
    for half in (0, 1):
        second.sibling_own(half)
        for which in range(3):
            second.sibling_other(which, half)
    for copy in shared:
        copy.wait_recv()

    heard(3)

    zs = nz // TP // PAIR
    members = nz // PAIR
    member = lax.div(z, PAIR)

    def make_term(turn):
        owner = lax.rem(lax.div(member, zs) + turn, TP)
        rows = columns[owner].reshape(zs * 64, PAIR * DP * PATCHES)
        result = jnp.dot(rows, dkv[...], preferred_element_type=F32)
        term[pl.ds(owner * zs, zs)] = result.reshape(zs, 64, KVC)

    lanes = ring_lanes(nz)
    height = 64 // PARTS

    def target(lane, step):
        way, base, size, _ = lane
        away = base + size - step
        return lax.rem((member + away, member + members - away)[way], members)

    def ring_copy(lane, step, piece):
        way, _, size, first = lane
        rows = pl.ds(piece * height, height)
        to = target(lane, step) * PAIR + parity if step == size - 1 else (z_after, z_before)[way]
        place = first + step
        return remote(
            ring_out.at[place, rows, :],
            ring_in.at[place, rows, :],
            ring_send.at[place * PARTS + piece],
            ring_recv.at[place * PARTS + piece],
            seq=to,
        )

    def ring_step(lane, step):
        place = lane[3] + step
        for piece in range(PARTS):
            rows = pl.ds(piece * height, height)
            total = term[target(lane, step), rows, :]
            if step:
                ring_copy(lane, step - 1, piece).wait_recv()
                total += ring_in[place - 1, rows, :].astype(F32)
            ring_out[place, rows, :] = total.astype(BF16)
            ring_copy(lane, step, piece).start()

    for turn in (4, 5):
        make_term(turn)
    for lane in lanes[:2]:
        ring_step(lane, 0)
    for turn in (3, 2, 6):
        make_term(turn)
    for lane in lanes[2:4]:
        ring_step(lane, 0)
    for turn in (1, 7, 0):
        make_term(turn)
    for lane in lanes[4:]:
        ring_step(lane, 0)
    for step in range(1, max(lane[2] for lane in lanes)):
        for lane in lanes:
            if step < lane[2]:
                ring_step(lane, step)

    total = term[member]
    for lane in lanes[::-1]:
        for piece in range(PARTS):
            ring_copy(lane, lane[2] - 1, piece).wait_recv()
        total += ring_in[lane[3] + lane[2] - 1].astype(F32)
    quarter[dp] = total.astype(BF16)
    last = []
    for steps in (2, 1, 3):
        copy = remote(
            quarter.at[dp],
            quarter.at[dp],
            last_send.at[steps - 1],
            last_recv.at[steps - 1],
            dp=lax.rem(dp + steps, DP),
        )
        copy.start()
        last.append(copy)

    gather.finish()
    second.finish()
    for copy in cross + halo + chain + shared:
        copy.wait_send()

    for lane in lanes:
        for step in range(lane[2]):
            for piece in range(PARTS):
                ring_copy(lane, step, piece).wait_send()
    out_att.wait()
    out_dq.wait()
    for steps in range(1, DP):
        source = lax.rem(dp + DP - steps, DP)
        remote(
            quarter.at[source],
            quarter.at[source],
            last_send.at[steps - 1],
            last_recv.at[steps - 1],
            dp=source,
        ).wait_recv()
    for copy in last:
        copy.wait_send()
    weight_out[...] = quarter[...].reshape(DP * 64, KVC).astype(F32)


def local(nz, queries, images, kv_weight, gate, cotangent, span_first, span_last):
    zs = nz // TP
    any_space = pl.BlockSpec(memory_space=pltpu.HBM)
    vmem = pl.BlockSpec(memory_space=pltpu.VMEM)
    smem = pl.BlockSpec(memory_space=pltpu.SMEM)
    dma = pltpu.SemaphoreType.DMA
    rows = REACH * PATCHES
    low = lambda *shape: pltpu.VMEM(shape, BF16)
    hbm = lambda array: pltpu.with_memory_space_constraint(array, pltpu.HBM)
    wide = lambda *shape: pltpu.VMEM(shape, F32)
    return pl.pallas_call(
        functools.partial(kernel, nz),
        out_shape=(
            jax.ShapeDtypeStruct(queries.shape, BF16),
            jax.ShapeDtypeStruct(queries.shape, BF16),
            jax.ShapeDtypeStruct((DP * 64, KVC), F32),
        ),
        in_specs=[any_space, any_space, any_space, smem, any_space, smem, smem],
        out_specs=(any_space, any_space, vmem),
        scratch_shapes=[
            low(TOKENS, SHARD),
            low(TOKENS, SHARD),
            low(TP * SHARD, KVC),
            low(TP, PATCHES, SHARD),
            wide(PATCHES, KVC),
            low(PAIR, zs // PAIR, DP, 64, PATCHES),
            low(TP, zs // PAIR, 64, PAIR * DP * PATCHES),
            low(HEAD_SIZE, SHARD),
            low(TOKENS, SHARD),
            low(HEAD_SIZE, SHARD),
            low(rows, HEAD_SIZE),
            low(rows, HEAD_SIZE),
            wide(HEADS, TOKENS, rows),
            wide(HEADS, TOKENS, rows),
            low(HEADS * TOKENS, rows),
            low(HEADS * TOKENS, rows),
            low(TOKENS, SHARD),
            low(TOKENS, SHARD),
            wide(REACH, 2, PATCHES, HEAD_SIZE),
            low(REACH - 1, 2, PATCHES, HEAD_SIZE),
            low(REACH - 1, 2, PATCHES, HEAD_SIZE),
            low(PAIR * DP * PATCHES, KVC),
            wide(nz // PAIR, 64, KVC),
            low(nz // PAIR - 1, 64, KVC),
            low(nz // PAIR - 1, 64, KVC),
            low(DP, 64, KVC),
            dma((7,)),
            dma((GATHER_COPIES,)),
            dma((GATHER_COPIES,)),
            dma((GATHER_COPIES,)),
            dma((GATHER_COPIES,)),
            dma((PAIR * DP - 1,)),
            dma((PAIR * DP - 1,)),
            dma((2 * (REACH - 1),)),
            dma((2 * (REACH - 1),)),
            dma((2 * (REACH - 1),)),
            dma((2 * (REACH - 1),)),
            dma((PAIR * DP - 1,)),
            dma((PAIR * DP - 1,)),
            dma(((nz // PAIR - 1) * PARTS,)),
            dma(((nz // PAIR - 1) * PARTS,)),
            dma((DP - 1,)),
            dma((DP - 1,)),
            pltpu.SemaphoreType.REGULAR((2 * len(GREETINGS),)),
        ],
        compiler_params=pltpu.CompilerParams(
            collective_id=0, has_side_effects=True, vmem_limit_bytes=48 * 1024 * 1024
        ),
        name="cross_attention",
    )(hbm(queries), hbm(images), hbm(kv_weight), gate, hbm(cotangent), span_first, span_last)


def solution(mesh):
    return jax.shard_map(
        functools.partial(local, mesh.shape["seq"]),
        mesh=mesh,
        in_specs=(
            P("dp", "seq", "tp"),
            P("dp", "seq", None, "tp"),
            P(None, "tp"),
            P(),
            P("dp", "seq", "tp"),
            P("dp", "seq"),
            P("dp", "seq"),
        ),
        out_specs=(P("dp", "seq", "tp"), P("dp", "seq", "tp"), P("seq", "tp")),
        check_vma=False,
    )
```
